128 devices in a mesh: rows: 32 (over x, y, core), feat: 4 (over z).
Axes of the slice: x: 4, y: 4, z: 4, core: 2. Of those that a mesh axis runs over, the one named last changes fastest.
Arguments:
- design: bfloat16 [8192, 65536], P('rows', 'feat')
- labels: int32 [8192], P('rows'), may hold values from -1 to 1, as said below
- start_position: float32 [16, 65536], P(None, 'feat')
- momenta: float32 [8, 4, 65536], P(None, None, 'feat'), may hold values from -6 to 6
- lag_offsets: int32 [8], replicated, may hold values from 0 to 2, as said below
- accept_bits: int32 [2, 16], replicated, may hold values 0 or 1
- step_sizes: float32 [8], replicated, may hold values from 0.1 to 0.3
Outputs:
- final_position: float32 [16, 65536], P(None, 'feat')
- final_momentum: float32 [16, 65536], P(None, 'feat')
- log_likelihood: float32 [2, 16], replicated
- distance: float32 [2, 8], replicated
The draws below stay inside these ranges and needn't reach their ends.
Inputs may be any that keep to these rules, and one draw needn't show every extreme that they name: `labels`: each entry is -1 or 1. `lag_offsets`: some pair has lag 0 and some pair has lag 2.
All inputs are finite; a program needn't handle non-finite values.
Results may differ from the reference program's by a relative error of at most 0.00043.
Values may be sent and summed in bfloat16 or wider, within the bound.
No kernel may reach another device: no remote copies, remote signals or barrier semaphores. Data moves between devices by JAX's collectives and lax.ppermute only.
A program may use at most 64 MiB of HBM per device.

```python
import math
import jax
import jax.numpy as jnp
from jax import lax

FEATURES = 65536
PAIRS = 8
TRANS = 2
LEAP = 5
MAXLAG = 2
CHAINS = 16
BANK = 4
ROWS = 8192


def draw_design(key, part):
    key_rows, key_cols, key_base = jax.random.split(jax.random.fold_in(key, 11), 3)
    rise = 1.0 + 2.0 * jnp.arange(ROWS, dtype=jnp.float32) / max(ROWS - 1, 1)
    row_scale = rise * jnp.exp(jax.random.uniform(key_rows, (ROWS,), minval=0.0, maxval=math.log(3.0)))
    col_scale = jnp.exp(jax.random.uniform(key_cols, (FEATURES,), minval=0.0, maxval=math.log(10.0)))
    base = jax.random.normal(key_base, (ROWS, FEATURES))
    row_moment = 8.0 / (2.0 * math.log(3.0))
    col_moment = 99.0 / (2.0 * math.log(10.0))
    factor = 2.0 / math.sqrt(FEATURES * (13.0 / 3.0) * row_moment * col_moment)
    return (base * row_scale[:, None] * col_scale[None, :] * factor).astype(jnp.bfloat16)


def draw_labels(key, part):
    coins = jax.random.randint(jax.random.fold_in(key, 23), (ROWS,), 0, 2)
    return (2 * coins - 1).astype(jnp.int32)


def draw_start_position(key, part):
    key_base = jax.random.fold_in(key, 37)
    rise = 1.0 + 2.0 * jnp.arange(FEATURES, dtype=jnp.float32) / max(FEATURES - 1, 1)
    base = jax.random.normal(key_base, (CHAINS, FEATURES))
    return (0.5 * base * rise[None, :]).astype(jnp.float32)


def draw_lag_offsets(key, part):
    key_values, key_place = jax.random.split(jax.random.fold_in(key, 41))
    values = jax.random.randint(key_values, (PAIRS,), 0, MAXLAG + 1)
    place = jax.random.randint(key_place, (), 0, PAIRS)
    slots = jnp.arange(PAIRS)
    values = jnp.where(slots == place, MAXLAG, values)
    values = jnp.where(slots == (place + 1) % PAIRS, 0, values)
    return values.astype(jnp.int32)


def place_ends(array, rng, least, top_value):
    longest = array.shape.index(max(array.shape))
    spots = []
    for shift in (0, 1):
        where = [jax.random.randint(jax.random.fold_in(rng, axis), (), 0, length) for axis, length in enumerate(array.shape)]
        where[longest] = (where[longest] + shift) % array.shape[longest]
        spots.append(tuple(where))
    return array.at[spots[0]].set(least).at[spots[1]].set(top_value)


def block_scale(key, extent, cuts, low, top_value):
    factor_of, own = 1.0, jax.random.fold_in(key, 6)
    for dim, parts in cuts:
        steps = jnp.exp(jax.random.uniform(jax.random.fold_in(own, dim), (parts,), jnp.float32, low / len(cuts), top_value / len(cuts)))
        factor_of = factor_of * jnp.repeat(steps, extent[dim] // parts).reshape([-1 if axis == dim else 1 for axis in range(len(extent))])
    return factor_of


def scatter_about(key, extent, deviation, bound, pieces=(), kind=jnp.bfloat16):
    drawn = deviation * jax.random.normal(key, extent, jnp.float32)
    if pieces:
        drawn = drawn * block_scale(key, extent, pieces, -0.22, 0.18)
    return jnp.clip(drawn, -bound, bound).astype(kind)


def setup_inputs(seed: int = 0) -> dict:
    keys = jax.random.split(jax.random.key(seed), 8)
    return {
        "design": draw_design(jax.random.fold_in(keys[7], 71), 0),
        "labels": draw_labels(jax.random.fold_in(keys[7], 71), 0),
        "start_position": draw_start_position(jax.random.fold_in(keys[7], 71), 0),
        "momenta": scatter_about(keys[3], (PAIRS, BANK, FEATURES), 1.0, 6.0, ((2, 4),), jnp.float32),
        "lag_offsets": draw_lag_offsets(jax.random.fold_in(keys[7], 71), 0),
        "accept_bits": place_ends((jax.random.randint(keys[5], (TRANS, CHAINS), 0, 2) < 1).astype(jnp.int32), jax.random.fold_in(keys[5], 1), 0, 1),
        "step_sizes": jnp.clip(jnp.exp(jax.random.uniform(keys[6], (PAIRS,), jnp.float32, math.log(0.1), math.log(0.3))), 0.1, 0.3),
    }


def gradient_at(design, label_signs, position):
    rounded = position.astype(jnp.bfloat16)
    margins = lax.dot_general(rounded, design, (((1,), (1,)), ((), ())), preferred_element_type=jnp.float32)
    weights = (label_signs * jax.nn.sigmoid(-label_signs * margins)).astype(jnp.bfloat16)
    summed = jnp.dot(weights, design, preferred_element_type=jnp.float32)
    return (margins, summed - position)

def reference(design, labels, start_position, momenta, lag_offsets, accept_bits, step_sizes):
    label_signs = labels.astype(jnp.float32)
    chain_steps = jnp.repeat(step_sizes, 2)[:, None]
    position = start_position
    margins, gradient = gradient_at(design, label_signs, position)
    likes = []
    distances = []
    momentum = position
    for transition in range(TRANS):
        leader_index = (transition + lag_offsets).astype(jnp.int32)
        leader = jnp.take_along_axis(momenta, leader_index[:, None, None], axis=1)[:, 0, :]
        trailer = momenta[:, transition, :]
        momentum = jnp.stack([leader, trailer], axis=1).reshape(CHAINS, FEATURES)
        momentum = momentum + 0.5 * chain_steps * gradient
        proposal = position
        new_gradient = gradient
        for leap_index in range(LEAP):
            proposal = proposal + chain_steps * momentum
            margins, new_gradient = gradient_at(design, label_signs, proposal)
            if leap_index + 1 < LEAP:
                momentum = momentum + chain_steps * new_gradient
            else:
                momentum = momentum + 0.5 * chain_steps * new_gradient
        likes.append(lax.optimization_barrier(jnp.sum(jax.nn.log_sigmoid(label_signs * margins), axis=1)) / ROWS)
        keep = (accept_bits[transition] == 1)[:, None]
        position = jnp.where(keep, proposal, position)
        gradient = jnp.where(keep, new_gradient, gradient)
        separation = position[0::2] - position[1::2]
        distances.append(jnp.sqrt(lax.optimization_barrier(jnp.sum(separation * separation, axis=1)) / FEATURES + 1e-06))
    return (position, momentum, jnp.stack(likes), jnp.stack(distances))
```

```python
import jax
import jax.numpy as jnp
from jax import lax
from jax.experimental import pallas as pl
from jax.experimental.pallas import tpu as pltpu
from jax.sharding import PartitionSpec as P

FEATURES = 65536
TRANS = 2
LEAP = 5
CHAINS = 16
EXTRA = 128
CHUNKS = 8

F32 = jnp.float32
BF16 = jnp.bfloat16
VMEM = pl.BlockSpec(memory_space=pltpu.VMEM)
ANY = pl.BlockSpec(memory_space=pl.ANY)


def params(mib):
    return pltpu.CompilerParams(vmem_limit_bytes=mib * 1024 * 1024)


def lane_iota():
    return lax.broadcasted_iota(jnp.int32, (CHAINS, EXTRA), 1)


def split3(column, first_lane):
    lanes = lane_iota() - first_lane
    high = column.astype(BF16).astype(F32)
    middle = (column - high).astype(BF16).astype(F32)
    low = column - high - middle
    zero = jnp.zeros((CHAINS, EXTRA), F32)
    out = jnp.where(lanes == 0, high, zero)
    out = jnp.where(lanes == 1, middle, out)
    return jnp.where(lanes == 2, low, out)


def margins_kernel(coefficients, design, extended):
    rows, width = design.shape
    blocked = coefficients.ndim == 3
    step = width // CHUNKS
    out_width = rows + (EXTRA if extended else 0)

    def body(coef_ref, design_ref, margins_ref, held_ref, sems):
        copies = [
            pltpu.make_async_copy(
                design_ref.at[:, pl.ds(i * step, step)],
                held_ref.at[:, pl.ds(i * step, step)],
                sems.at[i],
            )
            for i in range(CHUNKS)
        ]
        for copy in copies:
            copy.start()
        total = jnp.zeros((CHAINS, rows), F32)
        if extended:
            side = jnp.zeros((CHAINS, EXTRA), F32)
            block = coef_ref.shape[2] - EXTRA
            for b in range(coef_ref.shape[0]):
                side = side + coef_ref[b, :, block:].astype(F32)
            margins_ref[:, rows:] = side
        for i in range(CHUNKS):
            copies[i].wait()
            if blocked:
                block = coef_ref.shape[2] - (EXTRA if extended else 0)
                for j in range(step // block):
                    at = i * step + j * block
                    total = total + lax.dot_general(
                        coef_ref[at // block, :, :block],
                        held_ref[:, at : at + block],
                        (((1,), (1,)), ((), ())),
                        preferred_element_type=F32,
                    )
            else:
                total = total + lax.dot_general(
                    coef_ref[:, i * step : (i + 1) * step].astype(BF16),
                    held_ref[:, i * step : (i + 1) * step],
                    (((1,), (1,)), ((), ())),
                    preferred_element_type=F32,
                )
        margins_ref[:, :rows] = total

    return pl.pallas_call(
        body,
        in_specs=[VMEM, ANY],
        out_specs=[VMEM, VMEM],
        out_shape=[
            jax.ShapeDtypeStruct((CHAINS, out_width), F32),
            jax.ShapeDtypeStruct(design.shape, design.dtype),
        ],
        scratch_shapes=[pltpu.SemaphoreType.DMA((CHUNKS,))],
        compiler_params=params(16),
        cost_estimate=pl.CostEstimate(
            flops=2 * CHAINS * rows * width, bytes_accessed=2 * rows * width, transcendentals=0
        ),
        name="margins",
    )(coefficients, design)


def terms_kernel(partials, signs, held, blocks, likes, earlier_likes):
    rows, width = held.shape
    block = width // blocks
    extended = earlier_likes is not None
    total_width = partials[0].shape[1]
    out_block = block + (EXTRA if extended else 0)

    def body(*refs):
        own, one, two, three, sign_ref, held_ref = refs[:6]
        rest = list(refs[6:])
        earlier_ref = rest.pop(0) if extended else None
        out_ref = rest.pop(0)
        total = (own[...] + two[...]) + (one[...] + three[...])
        sign = sign_ref[...]
        signed = sign * total[:, :rows]
        weights = (sign * jax.nn.sigmoid(-signed)).astype(BF16)
        if likes:
            terms = jnp.minimum(signed, 0.0) - jnp.log1p(jnp.exp(-jnp.abs(signed)))
            like = jnp.sum(terms, axis=1, keepdims=True)
            if extended:
                side = split3(earlier_ref[...][:, :1], 0) + split3(like, 3)
                side = side.astype(BF16)
                for b in range(blocks):
                    out_ref[b, :, block:] = side
                rest[0][...] = total[:, rows:]
            else:
                rest[0][...] = jnp.broadcast_to(like, (CHAINS, EXTRA))
        group = 4
        for b in range(0, blocks, group):
            terms = lax.dot_general(
                weights,
                held_ref[:, b * block : (b + group) * block],
                (((1,), (0,)), ((), ())),
                preferred_element_type=F32,
            ).astype(BF16)
            for j in range(group):
                out_ref[b + j, :, :block] = terms[:, j * block : (j + 1) * block]

    args = list(partials) + [signs, held] + ([earlier_likes] if extended else [])
    outs = [jax.ShapeDtypeStruct((blocks, CHAINS, out_block), BF16)]
    if likes:
        outs.append(jax.ShapeDtypeStruct((CHAINS, EXTRA), F32))
    del total_width
    return pl.pallas_call(
        body,
        in_specs=[VMEM] * len(args),
        out_specs=[VMEM] * len(outs),
        out_shape=outs,
        compiler_params=params(16),
        cost_estimate=pl.CostEstimate(
            flops=2 * CHAINS * rows * width, bytes_accessed=2 * rows * width, transcendentals=0
        ),
        name="terms",
    )(*args)


def summed(ref, block):
    parts = [ref[b, :, :block].astype(F32) for b in range(ref.shape[0])]
    while len(parts) > 1:
        parts = [parts[i] + parts[i + 1] for i in range(0, len(parts), 2)]
    return parts[0]


def square_gap(position):
    gap = position - pltpu.roll(position, CHAINS - 1, 0)
    return jnp.sum(gap * gap, axis=1, keepdims=True)


def step_kernel(mode, arrived, state, blocks):
    names = list(state)
    block = 512
    wide = mode == "before_last"
    out_block = block + (EXTRA if wide else 0)
    outs = {"send": ((blocks, CHAINS, out_block), BF16)}
    slice_names = {
        "first": ["q", "p", "g0"],
        "mid": ["q", "p"],
        "turn": ["q", "p", "pos", "gap"],
        "before_last": ["q", "p"],
        "last": [],
    }[mode]
    for name in slice_names:
        outs[name] = ((CHAINS, EXTRA if name == "gap" else block), F32)
    if mode == "before_last":
        outs["ends"] = ((blocks, 2 * CHAINS, block), F32)
    if mode == "last":
        outs["likes"] = ((CHAINS, EXTRA), F32)

    def body(*refs):
        arrived_ref = refs[0]
        vals = {n: r[...] for n, r in zip(names, refs[1 : 1 + len(names)])}
        out = dict(zip(outs, refs[1 + len(names) :]))
        g = summed(arrived_ref, block)
        if mode == "last":
            side = jnp.zeros((CHAINS, EXTRA), F32)
            for b in range(blocks):
                side = side + arrived_ref[b, :, block:].astype(F32)
            out["likes"][...] = side
            send = g.astype(BF16)
            for b in range(blocks):
                out["send"][b] = send
            return
        h = vals["h"]
        if mode == "first":
            p = vals["mom"] + 0.5 * h * (g - vals["q"])
            q = vals["q"] + h * p
            out["g0"][...] = g
        elif mode == "turn":
            keep = vals["keep"] != 0.0
            pos = jnp.where(keep, vals["q"], vals["q0"])
            gradient = jnp.where(keep, g - vals["q"], vals["g0"] - vals["q0"])
            p = vals["mom"] + 0.5 * h * gradient
            q = pos + h * p
            out["pos"][...] = pos
            out["gap"][...] = jnp.broadcast_to(square_gap(pos), (CHAINS, EXTRA))
        else:
            p = vals["p"] + h * (g - vals["q"])
            q = vals["q"] + h * p
        out["q"][...] = q
        out["p"][...] = p
        send = q.astype(BF16)
        for b in range(blocks):
            out["send"][b, :, :block] = send
        if mode == "before_last":
            keep = vals["keep"] != 0.0
            pos = jnp.where(keep, q, vals["pos"])
            side = split3(vals["gap"][:, :1], 0) + split3(square_gap(pos), 3)
            side = side.astype(BF16)
            base = p - 0.5 * h * q
            for b in range(blocks):
                out["send"][b, :, block:] = side
                out["ends"][b, :CHAINS] = pos
                out["ends"][b, CHAINS:] = base

    result = pl.pallas_call(
        body,
        in_specs=[VMEM] * (1 + len(names)),
        out_specs=[VMEM] * len(outs),
        out_shape=[jax.ShapeDtypeStruct(*v) for v in outs.values()],
        compiler_params=params(16),
        name="step_" + mode,
    )(arrived, *state.values())
    return dict(zip(outs, result))


def finish_kernel(ends, arrived, half_step):
    blocks, _, block = arrived.shape
    group = 8

    def body(ends_ref, arrived_ref, half_ref, pos_ref, mom_ref):
        for b in range(group):
            cols = pl.ds(b * block, block)
            pos_ref[:, cols] = ends_ref[b, :CHAINS]
            mom_ref[:, cols] = ends_ref[b, CHAINS:] + half_ref[...] * arrived_ref[b].astype(F32)

    shape = jax.ShapeDtypeStruct((CHAINS, blocks * block), F32)
    out_spec = pl.BlockSpec((CHAINS, group * block), lambda i: (0, i))
    return pl.pallas_call(
        body,
        grid=(blocks // group,),
        in_specs=[
            pl.BlockSpec((group, 2 * CHAINS, block), lambda i: (i, 0, 0)),
            pl.BlockSpec((group, CHAINS, block), lambda i: (i, 0, 0)),
            pl.BlockSpec((CHAINS, block), lambda i: (0, 0)),
        ],
        out_specs=[out_spec, out_spec],
        out_shape=[shape, shape],
        compiler_params=params(16),
        name="finish",
    )(ends, arrived, half_step)


def on_device(design, labels, start_position, momenta, lag_offsets, accept_bits, step_sizes):
    rows, width = design.shape
    blocks = lax.axis_size("rows")
    ring = lax.axis_size("feat")
    block = width // blocks
    at = lax.axis_index("rows") * block
    signs = labels.astype(F32)[None, :]

    chain_steps = jnp.repeat(step_sizes, 2)[:, None]
    h = jnp.broadcast_to(chain_steps, (CHAINS, block))
    keeps = [
        jnp.broadcast_to(accept_bits[s].astype(F32)[:, None], (CHAINS, block)) for s in range(TRANS)
    ]
    start = lax.dynamic_slice_in_dim(start_position, at, block, 1)
    draws = lax.dynamic_slice_in_dim(momenta, at, block, 2)
    slots = jnp.arange(momenta.shape[1])
    moms = []
    for s in range(TRANS):
        chosen = slots[None, :] == (s + lag_offsets)[:, None]
        leader = jnp.sum(jnp.where(chosen[:, :, None], draws, 0.0), axis=1)
        moms.append(jnp.stack([leader, draws[:, s]], axis=1).reshape(CHAINS, block))

    def exchange(blocked):
        return lax.all_to_all(blocked, "rows", 0, 0)

    def around(margins):
        return [margins] + [
            lax.ppermute(margins, "feat", [(i, (i + k) % ring) for i in range(ring)])
            for k in range(1, ring)
        ]

    def terms_at(coefficients, likes=False, earlier=None):
        margins, held = margins_kernel(coefficients, design, earlier is not None)
        return terms_kernel(around(margins), signs, held, blocks, likes, earlier)

    (out,) = terms_at(start_position)
    now = step_kernel("first", exchange(out), {"q": start, "mom": moms[0], "h": h}, blocks)
    g0 = now["g0"]
    for _ in range(LEAP - 1):
        (out,) = terms_at(exchange(now["send"]))
        now = step_kernel("mid", exchange(out), {"q": now["q"], "p": now["p"], "h": h}, blocks)
    out, like = terms_at(exchange(now["send"]), likes=True)
    now = step_kernel(
        "turn",
        exchange(out),
        {"q": now["q"], "q0": start, "g0": g0, "mom": moms[1], "h": h, "keep": keeps[0]},
        blocks,
    )
    position, gap = now["pos"], now["gap"]
    for leap in range(LEAP - 1):
        (out,) = terms_at(exchange(now["send"]))
        state = {"q": now["q"], "p": now["p"], "h": h}
        if leap + 2 < LEAP:
            now = step_kernel("mid", exchange(out), state, blocks)
        else:
            state.update(pos=position, gap=gap, keep=keeps[1])
            now = step_kernel("before_last", exchange(out), state, blocks)
    gathered = exchange(now["send"])
    ends, gathered = lax.optimization_barrier((now["ends"], gathered))
    ends = exchange(ends)
    out, gaps = terms_at(gathered, likes=True, earlier=like)
    now = step_kernel("last", exchange(out), {}, blocks)
    final_position, final_momentum = finish_kernel(ends, exchange(now["send"]), 0.5 * h)
    likes = now["likes"][:, :6].reshape(CHAINS, 2, 3).sum(2).T
    squares = gaps[0::2, :6].reshape(CHAINS // 2, 2, 3).sum(2).T
    return (
        final_position,
        final_momentum,
        likes / (rows * blocks),
        jnp.sqrt(squares / FEATURES + 1e-06),
    )


def solution(mesh):
    return jax.shard_map(
        on_device,
        mesh=mesh,
        in_specs=(
            P("rows", "feat"),
            P("rows"),
            P(None, "feat"),
            P(None, None, "feat"),
            P(),
            P(),
            P(),
        ),
        out_specs=(P(None, "feat"), P(None, "feat"), P(), P()),
        check_vma=False,
    )
```

```python
import jax
import jax.numpy as jnp
from jax import lax
from jax.experimental import pallas as pl
from jax.experimental.pallas import tpu as pltpu
from jax.sharding import PartitionSpec as P

FEATURES = 65536
TRANS = 2
LEAP = 5
PAIRS = 8
CHAINS = 16
EXTRA = 128
CHUNKS = 8
GROUP = 4

F32 = jnp.float32
BF16 = jnp.bfloat16
VMEM = pl.BlockSpec(memory_space=pltpu.VMEM)
HBM = pl.BlockSpec(memory_space=pltpu.HBM)
SMEM = pl.BlockSpec(memory_space=pltpu.SMEM)
PARAMS = pltpu.CompilerParams(vmem_limit_bytes=6 * 1024 * 1024)
CROSS = (((1,), (1,)), ((), ()))


def call(body, name, ins, outs, scratch=(), flops=0):
    return pl.pallas_call(
        body,
        in_specs=[spec for _, spec in ins],
        out_specs=[VMEM] * len(outs),
        out_shape=[jax.ShapeDtypeStruct(*o) for o in outs],
        scratch_shapes=list(scratch),
        compiler_params=PARAMS,
        cost_estimate=pl.CostEstimate(flops=flops, bytes_accessed=flops // 16, transcendentals=0),
        name=name,
    )(*[a for a, _ in ins])


def vmem(*arrays):
    return [(a, VMEM) for a in arrays]


def first_margins(start, design):
    rows, width = design.shape
    step = width // CHUNKS

    def body(start_ref, design_ref, margins_ref, held_ref, sems):
        copies = []
        for i in range(CHUNKS):
            cols = pl.ds(i * step, step)
            copies.append(
                pltpu.make_async_copy(design_ref.at[:, cols], held_ref.at[:, cols], sems.at[i])
            )
            copies[-1].start()
        total = jnp.zeros((CHAINS, rows), F32)
        for i in range(CHUNKS):
            cols = slice(i * step, (i + 1) * step)
            copies[i].wait()
            total = total + lax.dot_general(
                start_ref[:, cols].astype(BF16), held_ref[:, cols], CROSS, preferred_element_type=F32
            )
        margins_ref[...] = total

    return call(
        body,
        "margins_start",
        [(start, VMEM), (design, HBM)],
        [((CHAINS, rows), F32), (design.shape, design.dtype)],
        [pltpu.SemaphoreType.DMA((CHUNKS,))],
        2 * CHAINS * rows * width,
    )


def draw_momenta(momenta, lag_offsets):
    _, _, width = momenta.shape

    def body(lag_ref, bank_ref, *out_refs):
        for s, out_ref in enumerate(out_refs):
            for k in range(PAIRS):
                out_ref[2 * k : 2 * k + 1] = bank_ref[k, pl.ds(s + lag_ref[k], 1)]
                out_ref[2 * k + 1 : 2 * k + 2] = bank_ref[k, s : s + 1]

    return call(
        body,
        "draw",
        [(lag_offsets, SMEM), (momenta, VMEM)],
        [((CHAINS, width), F32)] * TRANS,
    )


def square_gap(position):
    gap = position - pltpu.roll(position, CHAINS - 1, 0)
    return jnp.sum(gap * gap, axis=1, keepdims=True)


def margins_kernel(mode, held, arrived, h, state):
    rows, width = held.shape
    blocks, _, block = arrived.shape
    names = list(state)
    wide = ((CHAINS, width), F32)
    outs = {"margins": ((CHAINS, rows + (EXTRA if mode == "last" else 0)), F32), "q": wide, "p": wide}
    if mode == "turn":
        outs["pos"] = wide
        outs["gap"] = ((CHAINS, EXTRA), F32)
    if mode == "last":
        outs["pos"] = wide

    def body(held_ref, arrived_ref, h_ref, *refs):
        ins = dict(zip(names, refs))
        out = dict(zip(outs, refs[len(names) :]))
        h_col = h_ref[...]
        h_wide = jnp.broadcast_to(h_col[:, :1], (CHAINS, block))
        total = jnp.zeros((CHAINS, rows), F32)
        gap = jnp.zeros((CHAINS, 1), F32)
        if mode in ("turn", "last"):
            keep = jnp.broadcast_to(ins["keep"][:, :1], (CHAINS, block)) != 0.0
        for b in range(blocks):
            cols = slice(b * block, (b + 1) * block)
            g = arrived_ref[b].astype(F32)
            q = ins["q"][:, cols]
            if mode == "first":
                p = ins["mom"][:, cols] + 0.5 * h_wide * (g - q)
            elif mode == "turn":
                q0 = ins["q0"][:, cols]
                pos = jnp.where(keep, q, q0)
                gradient = jnp.where(keep, g - q, ins["g0"][b].astype(F32) - q0)
                p = ins["mom"][:, cols] + 0.5 * h_wide * gradient
                q = pos
                out["pos"][:, cols] = pos
                gap = gap + square_gap(pos)
            else:
                p = ins["p"][:, cols] + h_wide * (g - q)
            q = q + h_wide * p
            out["p"][:, cols] = p
            out["q"][:, cols] = q
            if mode == "last":
                pos = jnp.where(keep, q, ins["pos"][:, cols])
                out["pos"][:, cols] = pos
                gap = gap + square_gap(pos)
            total = total + lax.dot_general(
                q.astype(BF16), held_ref[:, cols], CROSS, preferred_element_type=F32
            )
        if mode == "turn":
            out["gap"][...] = jnp.broadcast_to(gap, (CHAINS, EXTRA))
        if mode == "last":
            lanes = lax.broadcasted_iota(jnp.int32, (CHAINS, EXTRA), 1)
            out["margins"][:, rows:] = jnp.where(lanes == 0, ins["gap"][...], gap)
        out["margins"][:, :rows] = total

    result = call(
        body,
        "margins_" + mode,
        vmem(held, arrived, h, *state.values()),
        list(outs.values()),
        flops=2 * CHAINS * rows * width,
    )
    return dict(zip(outs, result))


def split3(column, first_lane):
    lanes = lax.broadcasted_iota(jnp.int32, (CHAINS, EXTRA), 1) - first_lane
    high = column.astype(BF16).astype(F32)
    middle = (column - high).astype(BF16).astype(F32)
    low = column - high - middle
    out = jnp.where(lanes == 0, high, jnp.zeros((CHAINS, EXTRA), F32))
    out = jnp.where(lanes == 1, middle, out)
    return jnp.where(lanes == 2, low, out)


def terms_kernel(partials, signs, held, blocks, likes, earlier):
    rows, width = held.shape
    block = width // blocks
    extended = earlier is not None

    def body(*refs):
        own, one, two, three, sign_ref, held_ref = refs[:6]
        rest = list(refs[6:])
        earlier_ref = rest.pop(0) if extended else None
        out_ref = rest.pop(0)
        total = (own[...] + two[...]) + (one[...] + three[...])
        sign = sign_ref[...]
        signed = sign * total[:, :rows]
        weights = (sign * jax.nn.sigmoid(-signed)).astype(BF16)
        if likes:
            terms = jnp.minimum(signed, 0.0) - jnp.log1p(jnp.exp(-jnp.abs(signed)))
            like = jnp.sum(terms, axis=1, keepdims=True)
            if extended:
                side = split3(earlier_ref[...][:, :1], 0) + split3(like, 3)
                side = side.astype(BF16)
                for b in range(blocks):
                    out_ref[b, :, block:] = side
                rest[0][...] = total[:, rows:]
            else:
                rest[0][...] = jnp.broadcast_to(like, (CHAINS, EXTRA))
        for b in range(0, blocks, GROUP):
            terms = jnp.dot(
                weights,
                held_ref[:, b * block : (b + GROUP) * block],
                preferred_element_type=F32,
            ).astype(BF16)
            for j in range(GROUP):
                out_ref[b + j, :, :block] = terms[:, j * block : (j + 1) * block]

    outs = [((blocks, CHAINS, block + (EXTRA if extended else 0)), BF16)]
    if likes:
        outs.append(((CHAINS, EXTRA), F32))
    return call(
        body,
        "terms",
        vmem(*partials, signs, held, *([earlier] if extended else [])),
        outs,
        flops=2 * CHAINS * rows * width,
    )


def sum_kernel(arrived, residual, block, likes):
    blocks = arrived.shape[0]
    carried = residual is not None

    def body(*refs):
        arrived_ref = refs[0]
        send_ref, residual_ref = refs[2 if carried else 1 :][:2]
        parts = [arrived_ref[b, :, :block].astype(F32) for b in range(blocks)]
        while len(parts) > 1:
            parts = [parts[i] + parts[i + 1] for i in range(0, len(parts), 2)]
        exact = parts[0] + refs[1][...] if carried else parts[0]
        send = exact.astype(BF16)
        residual_ref[...] = exact - send.astype(F32)
        for b in range(blocks):
            send_ref[b] = send
        if likes:
            side = jnp.zeros((CHAINS, EXTRA), F32)
            for b in range(blocks):
                side = side + arrived_ref[b, :, block:].astype(F32)
            refs[-1][...] = side

    outs = [((blocks, CHAINS, block), BF16), ((CHAINS, block), F32)]
    if likes:
        outs.append(((CHAINS, EXTRA), F32))
    return call(body, "sum", vmem(arrived, *([residual] if carried else [])), outs)


def finish_kernel(arrived, h, p, q):
    blocks, _, block = arrived.shape

    def body(arrived_ref, h_ref, p_ref, q_ref, out_ref):
        half = 0.5 * jnp.broadcast_to(h_ref[...][:, :1], (CHAINS, block))
        for b in range(blocks):
            cols = slice(b * block, (b + 1) * block)
            out_ref[:, cols] = p_ref[:, cols] + half * (arrived_ref[b].astype(F32) - q_ref[:, cols])

    return call(body, "finish", vmem(arrived, h, p, q), [((CHAINS, blocks * block), F32)])[0]


def on_device(design, labels, start_position, momenta, lag_offsets, accept_bits, step_sizes):
    rows, width = design.shape
    blocks = lax.axis_size("rows")
    ring = lax.axis_size("feat")
    block = width // blocks
    signs = labels.astype(F32)[None, :]
    h = jnp.broadcast_to(jnp.repeat(step_sizes, 2)[:, None], (CHAINS, EXTRA))
    keeps = [
        jnp.broadcast_to(accept_bits[s].astype(F32)[:, None], (CHAINS, EXTRA)) for s in range(TRANS)
    ]
    moms = draw_momenta(momenta, lag_offsets)
    design, start, signs, h, keeps, moms = lax.optimization_barrier(
        (design, start_position, signs, h, keeps, moms)
    )

    def exchange(blocked):
        return lax.all_to_all(blocked, "rows", 0, 0)

    def around(margins):
        return [margins] + [
            lax.ppermute(margins, "feat", [(i, (i + k) % ring) for i in range(ring)])
            for k in range(1, ring)
        ]

    def gradient(margins, residual, likes=False, earlier=None):
        out, *side = terms_kernel(around(margins), signs, held, blocks, likes, earlier)
        send, residual, *totals = sum_kernel(exchange(out), residual, block, earlier is not None)
        return exchange(send), residual, side + totals

    margins, held = first_margins(start, design)
    g0, residual, _ = gradient(margins, None)
    g = g0
    now = {"q": start}
    for leap in range(LEAP):
        if leap == 0:
            now = margins_kernel("first", held, g, h, {"q": start, "mom": moms[0]})
        else:
            now = margins_kernel("mid", held, g, h, {"q": now["q"], "p": now["p"]})
        g, residual, side = gradient(now["margins"], residual, likes=leap + 1 == LEAP)
    (like,) = side
    for leap in range(LEAP):
        if leap == 0:
            state = {"q": now["q"], "q0": start, "g0": g0, "mom": moms[1], "keep": keeps[0]}
            now = margins_kernel("turn", held, g, h, state)
            position, gap = now["pos"], now["gap"]
        elif leap + 1 < LEAP:
            now = margins_kernel("mid", held, g, h, {"q": now["q"], "p": now["p"]})
        else:
            state = {"q": now["q"], "p": now["p"], "pos": position, "gap": gap, "keep": keeps[1]}
            now = margins_kernel("last", held, g, h, state)
        last = leap + 1 == LEAP
        g, residual, side = gradient(now["margins"], residual, last, like if last else None)
    gaps, likes = side
    momentum = finish_kernel(g, h, now["p"], now["q"])
    likes = likes[:, :6].reshape(CHAINS, 2, 3).sum(2).T
    squares = gaps[0::2, :2].T
    return (
        now["pos"],
        momentum,
        likes / (rows * blocks),
        jnp.sqrt(squares / FEATURES + 1e-06),
    )


def solution(mesh):
    return jax.shard_map(
        on_device,
        mesh=mesh,
        in_specs=(
            P("rows", "feat"),
            P("rows"),
            P(None, "feat"),
            P(None, None, "feat"),
            P(),
            P(),
            P(),
        ),
        out_specs=(P(None, "feat"), P(None, "feat"), P(), P()),
        check_vma=False,
    )
```

```python
import jax
import jax.numpy as jnp
from jax import lax
from jax.experimental import pallas as pl
from jax.experimental.pallas import tpu as pltpu
from jax.sharding import PartitionSpec as P

FEATURES = 65536
TRANS = 2
LEAP = 5
PAIRS = 8
CHAINS = 16
EXTRA = 128
CHUNKS = 4
GROUP = 4

F32 = jnp.float32
BF16 = jnp.bfloat16
VMEM = pl.BlockSpec(memory_space=pltpu.VMEM)
HBM = pl.BlockSpec(memory_space=pltpu.HBM)
SMEM = pl.BlockSpec(memory_space=pltpu.SMEM)
CROSS = (((1,), (1,)), ((), ()))


def limit(mib):
    return pltpu.CompilerParams(vmem_limit_bytes=mib * 1024 * 1024)


def call(body, name, ins, outs, scratch=(), flops=0, mib=6):
    return pl.pallas_call(
        body,
        in_specs=[spec for _, spec in ins],
        out_specs=[VMEM] * len(outs),
        out_shape=[jax.ShapeDtypeStruct(*o) for o in outs],
        scratch_shapes=list(scratch),
        compiler_params=limit(mib),
        cost_estimate=pl.CostEstimate(flops=flops, bytes_accessed=flops // 16, transcendentals=0),
        name=name,
    )(*[a for a, _ in ins])


def vmem(*arrays):
    return [(a, VMEM) for a in arrays]


def prepare(design, labels, start, momenta, lag_offsets, accept_bits, step_sizes):
    rows, width = design.shape
    half = width // 2
    step = half // CHUNKS
    slots = momenta.shape[1]

    def body(lag_ref, accept_ref, steps_ref, label_ref, start_ref, bank_ref, design_ref, *refs):
        margins_ref, own_ref, away_ref, q_ref, mom0_ref, mom1_ref, h_ref, keep0_ref, keep1_ref = refs[:9]
        far_ref, draws_ref, sems = refs[9:]
        core = lax.rem(lax.axis_index("rows"), 2)
        near = core * half
        far = (1 - core) * half
        count = [0]

        def fetch(source, target):
            copy = pltpu.make_async_copy(source, target, sems.at[count[0]])
            count[0] += 1
            copy.start()
            return copy

        def cols(offset, size):
            return pl.ds(pl.multiple_of(offset, step), size)

        first = [
            fetch(start_ref.at[:, cols(near, half)], q_ref),
            fetch(start_ref.at[:, cols(far, half)], far_ref),
        ]
        pieces = []
        for offset, target, coefs in ((far, away_ref, far_ref), (near, own_ref, q_ref)):
            for i in range(CHUNKS):
                here = slice(i * step, (i + 1) * step)
                copy = fetch(
                    design_ref.at[:, cols(offset + i * step, step)],
                    target.at[:, pl.ds(i * step, step)],
                )
                pieces.append((copy, target, coefs, here))
        bank_copy = fetch(bank_ref.at[:, :, cols(near, half)], draws_ref)
        row = lax.broadcasted_iota(jnp.int32, (CHAINS, EXTRA), 0)
        h = jnp.zeros((CHAINS, EXTRA), F32)
        for k in range(PAIRS):
            h = jnp.where(row // 2 == k, steps_ref[k], h)
        h_ref[...] = h
        for s, keep_ref in enumerate((keep0_ref, keep1_ref)):
            keep = jnp.zeros((CHAINS, EXTRA), F32)
            for k in range(CHAINS):
                keep = jnp.where(row == k, accept_ref[s, k].astype(F32), keep)
            keep_ref[...] = keep
        margins_ref[CHAINS:] = jnp.broadcast_to(label_ref[...].astype(F32), (8, rows))
        for copy in first:
            copy.wait()
        total = jnp.zeros((CHAINS, rows), F32)
        for copy, target, coefs, here in pieces:
            copy.wait()
            total = total + lax.dot_general(
                coefs[:, here].astype(BF16), target[:, here], CROSS, preferred_element_type=F32
            )
        margins_ref[:CHAINS] = total
        bank_copy.wait()
        for s, out_ref in enumerate((mom0_ref, mom1_ref)):
            for k in range(PAIRS):
                out_ref[2 * k : 2 * k + 1] = draws_ref[k, pl.ds(s + lag_ref[k], 1)]
                out_ref[2 * k + 1 : 2 * k + 2] = draws_ref[k, s : s + 1]

    small = ((CHAINS, EXTRA), F32)
    state = ((CHAINS, half), F32)
    piece = ((rows, half), design.dtype)
    return call(
        body,
        "prepare",
        [
            (lag_offsets, SMEM),
            (accept_bits, SMEM),
            (step_sizes, SMEM),
            (labels[None, :], VMEM),
            (start, HBM),
            (momenta, HBM),
            (design, HBM),
        ],
        [((CHAINS + 8, rows), F32), piece, piece, state, state, state, small, small, small],
        [
            pltpu.VMEM((CHAINS, half), F32),
            pltpu.VMEM((PAIRS, slots, half), F32),
            pltpu.SemaphoreType.DMA((3 + 2 * CHUNKS,)),
        ],
        2 * CHAINS * rows * width,
        38,
    )


def pair_start(mine, other):
    rows = mine.shape[1]

    def body(mine_ref, other_ref, margins_ref, sign_ref):
        margins_ref[:, :rows] = mine_ref[:CHAINS]
        margins_ref[:, rows:] = other_ref[:CHAINS]
        sign_ref[:, :rows] = mine_ref[CHAINS:]
        sign_ref[:, rows:] = other_ref[CHAINS:]

    outs = [((CHAINS, 2 * rows), F32), ((8, 2 * rows), F32)]
    return call(body, "pair_start", vmem(mine, other), outs)


def pair_sum(mine, other, rows):
    def body(mine_ref, other_ref, out_ref):
        out_ref[:, :rows] = mine_ref[:, :rows] + other_ref[:, rows : 2 * rows]
        out_ref[:, rows : 2 * rows] = mine_ref[:, rows : 2 * rows] + other_ref[:, :rows]
        if mine.shape[1] > 2 * rows:
            out_ref[:, 2 * rows :] = mine_ref[:, 2 * rows :] + other_ref[:, 2 * rows :]

    return call(body, "pair_sum", vmem(mine, other), [(mine.shape, F32)])[0]


def assemble(mine, other):
    half = mine.shape[1]

    def body(mine_ref, other_ref, out_ref, sems):
        core = lax.rem(lax.axis_index("rows"), 2)
        copies = []
        for i, (ref, at) in enumerate(((mine_ref, core), (other_ref, 1 - core))):
            cols = pl.ds(pl.multiple_of(at * half, half), half)
            copies.append(pltpu.make_async_copy(ref, out_ref.at[:, cols], sems.at[i]))
            copies[-1].start()
        for copy in copies:
            copy.wait()

    return pl.pallas_call(
        body,
        in_specs=[VMEM, VMEM],
        out_specs=HBM,
        out_shape=jax.ShapeDtypeStruct((CHAINS, 2 * half), F32),
        scratch_shapes=[pltpu.SemaphoreType.DMA((2,))],
        compiler_params=limit(6),
        name="assemble",
    )(mine, other)


def square_gap(position):
    gap = position - pltpu.roll(position, CHAINS - 1, 0)
    return jnp.sum(gap * gap, axis=1, keepdims=True)


def margins_kernel(mode, held, arrived, h, state):
    rows, width = held[0].shape
    blocks, _, block = arrived.shape
    names = list(state)
    wide = ((CHAINS, width), F32)
    outs = {"margins": ((CHAINS, 2 * rows + (EXTRA if mode == "last" else 0)), F32), "q": wide, "p": wide}
    if mode == "turn":
        outs["pos"] = wide
        outs["gap"] = ((CHAINS, EXTRA), F32)
    if mode == "last":
        outs["pos"] = wide

    def body(own_ref, other_ref, arrived_ref, h_ref, *refs):
        ins = dict(zip(names, refs))
        out = dict(zip(outs, refs[len(names) :]))
        h_col = h_ref[...]
        h_wide = jnp.broadcast_to(h_col[:, :1], (CHAINS, block))
        total = [jnp.zeros((CHAINS, rows), F32)] * 2
        gap = jnp.zeros((CHAINS, 1), F32)
        if mode in ("turn", "last"):
            keep = jnp.broadcast_to(ins["keep"][:, :1], (CHAINS, block)) != 0.0
        for b in range(blocks):
            cols = slice(b * block, (b + 1) * block)
            g = arrived_ref[b].astype(F32)
            q = ins["q"][:, cols]
            if mode == "first":
                p = ins["mom"][:, cols] + 0.5 * h_wide * (g - q)
            elif mode == "turn":
                q0 = ins["q0"][:, cols]
                pos = jnp.where(keep, q, q0)
                gradient = jnp.where(keep, g - q, ins["g0"][b].astype(F32) - q0)
                p = ins["mom"][:, cols] + 0.5 * h_wide * gradient
                q = pos
                out["pos"][:, cols] = pos
                gap = gap + square_gap(pos)
            else:
                p = ins["p"][:, cols] + h_wide * (g - q)
            q = q + h_wide * p
            out["p"][:, cols] = p
            out["q"][:, cols] = q
            if mode == "last":
                pos = jnp.where(keep, q, ins["pos"][:, cols])
                out["pos"][:, cols] = pos
                gap = gap + square_gap(pos)
            rounded = q.astype(BF16)
            for i, ref in enumerate((own_ref, other_ref)):
                total[i] = total[i] + lax.dot_general(
                    rounded, ref[:, cols], CROSS, preferred_element_type=F32
                )
        if mode == "turn":
            out["gap"][...] = jnp.broadcast_to(gap, (CHAINS, EXTRA))
        if mode == "last":
            lanes = lax.broadcasted_iota(jnp.int32, (CHAINS, EXTRA), 1)
            out["margins"][:, 2 * rows :] = jnp.where(lanes == 0, ins["gap"][...], gap)
        out["margins"][:, :rows] = total[0]
        out["margins"][:, rows : 2 * rows] = total[1]

    result = call(
        body,
        "margins_" + mode,
        vmem(*held, arrived, h, *state.values()),
        list(outs.values()),
        flops=4 * CHAINS * rows * width,
    )
    return dict(zip(outs, result))


def split3(column, first_lane):
    lanes = lax.broadcasted_iota(jnp.int32, (CHAINS, EXTRA), 1) - first_lane
    high = column.astype(BF16).astype(F32)
    middle = (column - high).astype(BF16).astype(F32)
    low = column - high - middle
    out = jnp.where(lanes == 0, high, jnp.zeros((CHAINS, EXTRA), F32))
    out = jnp.where(lanes == 1, middle, out)
    return jnp.where(lanes == 2, low, out)


def terms_kernel(partials, signs, held, blocks, likes, earlier):
    rows, width = held[0].shape
    block = width // blocks
    extended = earlier is not None

    def body(*refs):
        own, one, two, three, sign_ref, near_ref, far_ref = refs[:7]
        rest = list(refs[7:])
        earlier_ref = rest.pop(0) if extended else None
        out_ref = rest.pop(0)
        total = (own[...] + two[...]) + (one[...] + three[...])
        sign = sign_ref[:1]
        signed = sign * total[:, : 2 * rows]
        weights = (sign * jax.nn.sigmoid(-signed)).astype(BF16)
        if likes:
            terms = jnp.minimum(signed, 0.0) - jnp.log1p(jnp.exp(-jnp.abs(signed)))
            like = jnp.sum(terms, axis=1, keepdims=True)
            if extended:
                side = split3(earlier_ref[...][:, :1], 0) + split3(like, 3)
                side = side.astype(BF16)
                for b in range(blocks):
                    out_ref[b, :, block:] = side
                rest[0][...] = total[:, 2 * rows :]
            else:
                rest[0][...] = jnp.broadcast_to(like, (CHAINS, EXTRA))
        for b in range(0, blocks, GROUP):
            cols = slice(b * block, (b + GROUP) * block)
            terms = jnp.dot(weights[:, :rows], near_ref[:, cols], preferred_element_type=F32)
            terms = terms + jnp.dot(weights[:, rows:], far_ref[:, cols], preferred_element_type=F32)
            terms = terms.astype(BF16)
            for j in range(GROUP):
                out_ref[b + j, :, :block] = terms[:, j * block : (j + 1) * block]

    outs = [((blocks, CHAINS, block + (EXTRA if extended else 0)), BF16)]
    if likes:
        outs.append(((CHAINS, EXTRA), F32))
    return call(
        body,
        "terms",
        vmem(*partials, signs, *held, *([earlier] if extended else [])),
        outs,
        flops=4 * CHAINS * rows * width,
    )


def sum_kernel(arrived, residual, block, likes):
    blocks = arrived.shape[0]
    carried = residual is not None

    def body(*refs):
        arrived_ref = refs[0]
        send_ref, residual_ref = refs[2 if carried else 1 :][:2]
        parts = [arrived_ref[b, :, :block].astype(F32) for b in range(blocks)]
        while len(parts) > 1:
            parts = [parts[i] + parts[i + 1] for i in range(0, len(parts), 2)]
        exact = parts[0] + refs[1][...] if carried else parts[0]
        send = exact.astype(BF16)
        residual_ref[...] = exact - send.astype(F32)
        for b in range(blocks):
            send_ref[b] = send
        if likes:
            side = jnp.zeros((CHAINS, EXTRA), F32)
            for b in range(blocks):
                side = side + arrived_ref[b, :, block:].astype(F32)
            refs[-1][...] = side

    outs = [((blocks, CHAINS, block), BF16), ((CHAINS, block), F32)]
    if likes:
        outs.append(((CHAINS, EXTRA), F32))
    return call(body, "sum", vmem(arrived, *([residual] if carried else [])), outs)


def finish_kernel(arrived, h, p, q):
    blocks, _, block = arrived.shape

    def body(arrived_ref, h_ref, p_ref, q_ref, out_ref):
        half = 0.5 * jnp.broadcast_to(h_ref[...][:, :1], (CHAINS, block))
        for b in range(blocks):
            cols = slice(b * block, (b + 1) * block)
            out_ref[:, cols] = p_ref[:, cols] + half * (arrived_ref[b].astype(F32) - q_ref[:, cols])

    return call(body, "finish", vmem(arrived, h, p, q), [((CHAINS, blocks * block), F32)])[0]


def on_device(design, labels, start_position, momenta, lag_offsets, accept_bits, step_sizes):
    rows, _ = design.shape
    devices = lax.axis_size("rows")
    ring = lax.axis_size("feat")
    blocks = devices // 2
    chips = [[2 * k + core for k in range(blocks)] for core in range(2)]
    swap = [(i, i ^ 1) for i in range(devices)]

    def exchange(blocked):
        return lax.all_to_all(blocked, "rows", 0, 0, axis_index_groups=chips)

    def across(value):
        return lax.ppermute(value, "rows", swap)

    def around(margins):
        moved = {
            k: lax.ppermute(margins, "feat", [(i, (i + k) % ring) for i in range(ring)])
            for k in (1, 3, 2)
        }
        return [margins, moved[1], moved[2], moved[3]]

    def gradient(margins, residual, likes=False, earlier=None):
        out, *side = terms_kernel(around(margins), signs, held, blocks, likes, earlier)
        block = out.shape[2] - (EXTRA if earlier is not None else 0)
        send, residual, *totals = sum_kernel(exchange(out), residual, block, earlier is not None)
        return exchange(send), residual, side + totals

    def paired(margins):
        return pair_sum(margins, across(margins), rows)

    margins, own, away, start, mom0, mom1, h, keep0, keep1 = prepare(
        design, labels, start_position, momenta, lag_offsets, accept_bits, step_sizes
    )
    margins, signs = pair_start(margins, across(margins))
    held = (own, across(away))
    g0, residual, _ = gradient(margins, None)
    g = g0
    now = {"q": start}
    for leap in range(LEAP):
        if leap == 0:
            now = margins_kernel("first", held, g, h, {"q": start, "mom": mom0})
        else:
            now = margins_kernel("mid", held, g, h, {"q": now["q"], "p": now["p"]})
        g, residual, side = gradient(paired(now["margins"]), residual, likes=leap + 1 == LEAP)
    (like,) = side
    for leap in range(LEAP):
        last = leap + 1 == LEAP
        if leap == 0:
            state = {"q": now["q"], "q0": start, "g0": g0, "mom": mom1, "keep": keep0}
            now = margins_kernel("turn", held, g, h, state)
            position, gap = now["pos"], now["gap"]
        elif not last:
            now = margins_kernel("mid", held, g, h, {"q": now["q"], "p": now["p"]})
        else:
            state = {"q": now["q"], "p": now["p"], "pos": position, "gap": gap, "keep": keep1}
            now = margins_kernel("last", held, g, h, state)
        g, residual, side = gradient(paired(now["margins"]), residual, last, like if last else None)
    gaps, likes = side
    momentum = finish_kernel(g, h, now["p"], now["q"])
    likes = likes[:, :6].reshape(CHAINS, 2, 3).sum(2).T
    squares = gaps[0::2, :2].T
    return (
        assemble(now["pos"], across(now["pos"])),
        assemble(momentum, across(momentum)),
        likes / (rows * devices),
        jnp.sqrt(squares / FEATURES + 1e-06),
    )


def solution(mesh):
    return jax.shard_map(
        on_device,
        mesh=mesh,
        in_specs=(
            P("rows", "feat"),
            P("rows"),
            P(None, "feat"),
            P(None, None, "feat"),
            P(),
            P(),
            P(),
        ),
        out_specs=(P(None, "feat"), P(None, "feat"), P(), P()),
        check_vma=False,
    )
```

```python
import jax
import jax.numpy as jnp
from jax import lax
from jax.experimental import pallas as pl
from jax.experimental.pallas import tpu as pltpu
from jax.sharding import PartitionSpec as P

FEATURES = 65536
TRANS = 2
LEAP = 5
PAIRS = 8
CHAINS = 16
EXTRA = 128
CHUNKS = 4
GROUP = 4
WIDE = 8

F32 = jnp.float32
BF16 = jnp.bfloat16
VMEM = pl.BlockSpec(memory_space=pltpu.VMEM)
HBM = pl.BlockSpec(memory_space=pltpu.HBM)
SMEM = pl.BlockSpec(memory_space=pltpu.SMEM)
CROSS = (((1,), (1,)), ((), ()))


def limit(mib):
    return pltpu.CompilerParams(vmem_limit_bytes=mib * 1024 * 1024)


def call(body, name, ins, outs, scratch=(), flops=0, mib=6):
    return pl.pallas_call(
        body,
        in_specs=[spec for _, spec in ins],
        out_specs=[VMEM] * len(outs),
        out_shape=[jax.ShapeDtypeStruct(*o) for o in outs],
        scratch_shapes=list(scratch),
        compiler_params=limit(mib),
        cost_estimate=pl.CostEstimate(flops=flops, bytes_accessed=flops // 16, transcendentals=0),
        name=name,
    )(*[a for a, _ in ins])


def vmem(*arrays):
    return [(a, VMEM) for a in arrays]


def prepare(design, start):
    rows, width = design.shape
    half = width // 2
    step = half // CHUNKS

    def body(start_ref, design_ref, margins_ref, own_ref, away_ref, q_ref, far_ref, sems):
        core = lax.rem(lax.axis_index("rows"), 2)
        near = core * half
        far = (1 - core) * half
        count = [0]

        def fetch(source, target):
            copy = pltpu.make_async_copy(source, target, sems.at[count[0]])
            count[0] += 1
            copy.start()
            return copy

        def cols(offset, size):
            return pl.ds(pl.multiple_of(offset, step), size)

        first = [
            fetch(start_ref.at[:, cols(far, half)], far_ref),
            fetch(start_ref.at[:, cols(near, half)], q_ref),
        ]
        pieces = []
        for offset, target, coefs in ((far, away_ref, far_ref), (near, own_ref, q_ref)):
            for i in range(CHUNKS):
                here = slice(i * step, (i + 1) * step)
                copy = fetch(
                    design_ref.at[:, cols(offset + i * step, step)],
                    target.at[:, pl.ds(i * step, step)],
                )
                pieces.append((copy, target, coefs, here))
        for copy in first:
            copy.wait()
        total = jnp.zeros((CHAINS, rows), F32)
        for copy, target, coefs, here in pieces:
            copy.wait()
            total = total + lax.dot_general(
                coefs[:, here].astype(BF16), target[:, here], CROSS, preferred_element_type=F32
            )
        margins_ref[...] = total

    piece = ((rows, half), design.dtype)
    return call(
        body,
        "prepare",
        [(start, HBM), (design, HBM)],
        [((CHAINS, rows), F32), piece, piece, ((CHAINS, half), F32)],
        [pltpu.VMEM((CHAINS, half), F32), pltpu.SemaphoreType.DMA((2 + 2 * CHUNKS,))],
        2 * CHAINS * rows * width,
        38,
    )


def draw(labels, momenta, lag_offsets, accept_bits, step_sizes):
    rows = labels.shape[0]
    slots, width = momenta.shape[1:]
    half = width // 2

    def body(lag_ref, accept_ref, steps_ref, label_ref, bank_ref, *refs):
        mom0_ref, mom1_ref, h_ref, keep0_ref, keep1_ref, sign_ref, draws_ref, sem = refs
        core = lax.rem(lax.axis_index("rows"), 2)
        cols = pl.ds(pl.multiple_of(core * half, half), half)
        copy = pltpu.make_async_copy(bank_ref.at[:, :, cols], draws_ref, sem)
        copy.start()
        row = lax.broadcasted_iota(jnp.int32, (CHAINS, EXTRA), 0)
        h = jnp.zeros((CHAINS, EXTRA), F32)
        for k in range(PAIRS):
            h = jnp.where(row // 2 == k, steps_ref[k], h)
        h_ref[...] = h
        for s, keep_ref in enumerate((keep0_ref, keep1_ref)):
            keep = jnp.zeros((CHAINS, EXTRA), F32)
            for k in range(CHAINS):
                keep = jnp.where(row == k, accept_ref[s, k].astype(F32), keep)
            keep_ref[...] = keep
        sign_ref[...] = jnp.broadcast_to(label_ref[...].astype(F32), (8, rows))
        copy.wait()
        for s, out_ref in enumerate((mom0_ref, mom1_ref)):
            for k in range(PAIRS):
                out_ref[2 * k : 2 * k + 1] = draws_ref[k, pl.ds(s + lag_ref[k], 1)]
                out_ref[2 * k + 1 : 2 * k + 2] = draws_ref[k, s : s + 1]

    small = ((CHAINS, EXTRA), F32)
    state = ((CHAINS, half), F32)
    return call(
        body,
        "draw",
        [
            (lag_offsets, SMEM),
            (accept_bits, SMEM),
            (step_sizes, SMEM),
            (labels[None, :], VMEM),
            (momenta, HBM),
        ],
        [state, state, small, small, small, ((8, rows), F32)],
        [pltpu.VMEM((PAIRS, slots, half), F32), pltpu.SemaphoreType.DMA],
        0,
        8,
    )


def pair_start(mine, other):
    rows = mine.shape[1]

    def body(mine_ref, other_ref, margins_ref):
        margins_ref[:, :rows] = mine_ref[...]
        margins_ref[:, rows:] = other_ref[...]

    return call(body, "pair_start", vmem(mine, other), [((CHAINS, 2 * rows), F32)])[0]


def pair_sum(mine, other, rows):
    def body(mine_ref, other_ref, out_ref):
        out_ref[:, :rows] = mine_ref[:, :rows] + other_ref[:, rows : 2 * rows]
        out_ref[:, rows : 2 * rows] = mine_ref[:, rows : 2 * rows] + other_ref[:, :rows]
        if mine.shape[1] > 2 * rows:
            out_ref[:, 2 * rows :] = mine_ref[:, 2 * rows :] + other_ref[:, 2 * rows :]

    return call(body, "pair_sum", vmem(mine, other), [(mine.shape, F32)])[0]


def assemble(mine, other):
    half = mine.shape[1]

    def body(mine_ref, other_ref, out_ref, sems):
        core = lax.rem(lax.axis_index("rows"), 2)
        copies = []
        for i, (ref, at) in enumerate(((mine_ref, core), (other_ref, 1 - core))):
            cols = pl.ds(pl.multiple_of(at * half, half), half)
            copies.append(pltpu.make_async_copy(ref, out_ref.at[:, cols], sems.at[i]))
            copies[-1].start()
        for copy in copies:
            copy.wait()

    return pl.pallas_call(
        body,
        in_specs=[VMEM, VMEM],
        out_specs=HBM,
        out_shape=jax.ShapeDtypeStruct((CHAINS, 2 * half), F32),
        scratch_shapes=[pltpu.SemaphoreType.DMA((2,))],
        compiler_params=limit(6),
        name="assemble",
    )(mine, other)


def square_gap(position):
    gap = position - pltpu.roll(position, CHAINS - 1, 0)
    return jnp.sum(gap * gap, axis=1, keepdims=True)


def margins_kernel(mode, held, arrived, h, state):
    rows, width = held[0].shape
    blocks, _, block = arrived.shape
    names = list(state)
    wide = ((CHAINS, width), F32)
    outs = {"margins": ((CHAINS, 2 * rows + (EXTRA if mode == "last" else 0)), F32), "q": wide, "p": wide}
    if mode == "turn":
        outs["pos"] = wide
        outs["gap"] = ((CHAINS, EXTRA), F32)
    if mode == "last":
        outs["pos"] = wide

    def body(own_ref, other_ref, arrived_ref, h_ref, *refs):
        ins = dict(zip(names, refs))
        out = dict(zip(outs, refs[len(names) :]))
        h_col = h_ref[...]
        h_wide = jnp.broadcast_to(h_col[:, :1], (CHAINS, block))
        if mode in ("turn", "last"):
            keep = jnp.broadcast_to(ins["keep"][:, :1], (CHAINS, block)) != 0.0

        def one(b, cols, own, other, gap):
            g = arrived_ref[b].astype(F32)
            q = ins["q"][:, cols]
            if mode == "first":
                p = ins["mom"][:, cols] + 0.5 * h_wide * (g - q)
            elif mode == "turn":
                q0 = ins["q0"][:, cols]
                pos = jnp.where(keep, q, q0)
                gradient = jnp.where(keep, g - q, ins["g0"][b].astype(F32) - q0)
                p = ins["mom"][:, cols] + 0.5 * h_wide * gradient
                q = pos
                out["pos"][:, cols] = pos
                gap = gap + square_gap(pos)
            else:
                p = ins["p"][:, cols] + h_wide * (g - q)
            q = q + h_wide * p
            out["p"][:, cols] = p
            out["q"][:, cols] = q
            if mode == "last":
                pos = jnp.where(keep, q, ins["pos"][:, cols])
                out["pos"][:, cols] = pos
                gap = gap + square_gap(pos)
            rounded = q.astype(BF16)
            own = own + lax.dot_general(
                rounded, own_ref[:, cols], CROSS, preferred_element_type=F32
            )
            other = other + lax.dot_general(
                rounded, other_ref[:, cols], CROSS, preferred_element_type=F32
            )
            return own, other, gap

        def group(i, carry):
            for j in range(GROUP):
                b = i * GROUP + j
                carry = one(b, pl.ds(pl.multiple_of(b * block, block), block), *carry)
            return carry

        zero = jnp.zeros((CHAINS, rows), F32)
        *total, gap = lax.fori_loop(
            0, blocks // GROUP, group, (zero, zero, jnp.zeros((CHAINS, 1), F32))
        )
        if mode == "turn":
            out["gap"][...] = jnp.broadcast_to(gap, (CHAINS, EXTRA))
        if mode == "last":
            lanes = lax.broadcasted_iota(jnp.int32, (CHAINS, EXTRA), 1)
            out["margins"][:, 2 * rows :] = jnp.where(lanes == 0, ins["gap"][...], gap)
        out["margins"][:, :rows] = total[0]
        out["margins"][:, rows : 2 * rows] = total[1]

    result = call(
        body,
        "margins_" + mode,
        vmem(*held, arrived, h, *state.values()),
        list(outs.values()),
        flops=4 * CHAINS * rows * width,
    )
    return dict(zip(outs, result))


def split3(column, first_lane):
    lanes = lax.broadcasted_iota(jnp.int32, (CHAINS, EXTRA), 1) - first_lane
    high = column.astype(BF16).astype(F32)
    middle = (column - high).astype(BF16).astype(F32)
    low = column - high - middle
    out = jnp.where(lanes == 0, high, jnp.zeros((CHAINS, EXTRA), F32))
    out = jnp.where(lanes == 1, middle, out)
    return jnp.where(lanes == 2, low, out)


def terms_kernel(partials, signs, held, blocks, likes, earlier):
    rows, width = held[0].shape
    block = width // blocks
    extended = earlier is not None

    def body(*refs):
        own, one, two, three, mine_ref, theirs_ref, near_ref, far_ref = refs[:8]
        rest = list(refs[8:])
        earlier_ref = rest.pop(0) if extended else None
        out_ref = rest.pop(0)
        total = (own[...] + two[...]) + (one[...] + three[...])
        sign = jnp.concatenate([mine_ref[:1], theirs_ref[:1]], axis=1)
        signed = sign * total[:, : 2 * rows]
        weights = (sign * jax.nn.sigmoid(-signed)).astype(BF16)
        if likes:
            terms = jnp.minimum(signed, 0.0) - jnp.log1p(jnp.exp(-jnp.abs(signed)))
            like = jnp.sum(terms, axis=1, keepdims=True)
            if extended:
                side = split3(earlier_ref[...][:, :1], 0) + split3(like, 3)
                side = side.astype(BF16)
                for b in range(blocks):
                    out_ref[b, :, block:] = side
                squares = total[:, 2 * rows :].T[:2]
                chain = lax.broadcasted_iota(jnp.int32, (CHAINS, PAIRS), 0)
                pair = lax.broadcasted_iota(jnp.int32, (CHAINS, PAIRS), 1)
                leaders = (chain == 2 * pair).astype(F32)
                picked = jnp.dot(
                    squares, leaders, precision=lax.Precision.HIGHEST, preferred_element_type=F32
                )
                rest[0][...] = jnp.sqrt(picked / FEATURES + 1e-06)
            else:
                rest[0][...] = jnp.broadcast_to(like, (CHAINS, EXTRA))
        def group(i, carry):
            for j in range(WIDE):
                b = i * WIDE + j
                cols = pl.ds(pl.multiple_of(b * block, block), block)
                terms = jnp.dot(weights[:, :rows], near_ref[:, cols], preferred_element_type=F32)
                far = jnp.dot(weights[:, rows:], far_ref[:, cols], preferred_element_type=F32)
                out_ref[b, :, :block] = (terms + far).astype(BF16)
            return carry

        lax.fori_loop(0, blocks // WIDE, group, 0)

    outs = [((blocks, CHAINS, block + (EXTRA if extended else 0)), BF16)]
    if likes:
        outs.append(((TRANS, PAIRS) if extended else (CHAINS, EXTRA), F32))
    return call(
        body,
        "terms",
        vmem(*partials, *signs, *held, *([earlier] if extended else [])),
        outs,
        flops=4 * CHAINS * rows * width,
    )


def sum_kernel(arrived, residual, block, observations):
    blocks = arrived.shape[0]
    carried = residual is not None

    def body(*refs):
        arrived_ref = refs[0]
        send_ref, residual_ref = refs[2 if carried else 1 :][:2]
        parts = [arrived_ref[b, :, :block].astype(F32) for b in range(blocks)]
        while len(parts) > 1:
            parts = [parts[i] + parts[i + 1] for i in range(0, len(parts), 2)]
        exact = parts[0] + refs[1][...] if carried else parts[0]
        send = exact.astype(BF16)
        residual_ref[...] = exact - send.astype(F32)
        for b in range(blocks):
            send_ref[b] = send
        if observations:
            side = jnp.zeros((CHAINS, EXTRA), F32)
            for b in range(blocks):
                side = side + arrived_ref[b, :, block:].astype(F32)
            side = side.T
            for s in range(TRANS):
                like = (side[3 * s : 3 * s + 1] + side[3 * s + 1 : 3 * s + 2]) + side[3 * s + 2 : 3 * s + 3]
                refs[-1][s : s + 1] = like / observations

    outs = [((blocks, CHAINS, block), BF16), ((CHAINS, block), F32)]
    if observations:
        outs.append(((TRANS, CHAINS), F32))
    return call(body, "sum", vmem(arrived, *([residual] if carried else [])), outs)


def finish_kernel(arrived, h, p, q):
    blocks, _, block = arrived.shape

    def body(arrived_ref, h_ref, p_ref, q_ref, out_ref):
        half = 0.5 * jnp.broadcast_to(h_ref[...][:, :1], (CHAINS, block))
        for b in range(blocks):
            cols = slice(b * block, (b + 1) * block)
            out_ref[:, cols] = p_ref[:, cols] + half * (arrived_ref[b].astype(F32) - q_ref[:, cols])

    return call(body, "finish", vmem(arrived, h, p, q), [((CHAINS, blocks * block), F32)])[0]


def on_device(design, labels, start_position, momenta, lag_offsets, accept_bits, step_sizes):
    rows, _ = design.shape
    devices = lax.axis_size("rows")
    ring = lax.axis_size("feat")
    blocks = devices // 2
    chips = [[2 * k + core for k in range(blocks)] for core in range(2)]
    swap = [(i, i ^ 1) for i in range(devices)]

    def exchange(blocked):
        return lax.all_to_all(blocked, "rows", 0, 0, axis_index_groups=chips)

    def across(value):
        return lax.ppermute(value, "rows", swap)

    def around(margins):
        moved = {
            k: lax.ppermute(margins, "feat", [(i, (i + k) % ring) for i in range(ring)])
            for k in (1, 3, 2)
        }
        return [margins, moved[1], moved[2], moved[3]]

    def gradient(margins, residual, likes=False, earlier=None):
        last = earlier is not None
        out, *side = terms_kernel(around(margins), signs, held, blocks, likes, earlier)
        block = out.shape[2] - (EXTRA if last else 0)
        send, residual, *totals = sum_kernel(
            exchange(out), residual, block, rows * devices if last else 0
        )
        return exchange(send), residual, side + totals

    def paired(margins):
        return pair_sum(margins, across(margins), rows)

    margins, own, away, start = prepare(design, start_position)
    swapped = across(margins)
    away, swapped = lax.optimization_barrier((away, swapped))
    margins = pair_start(margins, swapped)
    held = (own, across(away))
    mom0, mom1, h, keep0, keep1, sign = draw(labels, momenta, lag_offsets, accept_bits, step_sizes)
    signs = (sign, across(sign))
    g0, residual, _ = gradient(margins, None)
    g = g0
    now = {"q": start}
    for leap in range(LEAP):
        if leap == 0:
            now = margins_kernel("first", held, g, h, {"q": start, "mom": mom0})
        else:
            now = margins_kernel("mid", held, g, h, {"q": now["q"], "p": now["p"]})
        g, residual, side = gradient(paired(now["margins"]), residual, likes=leap + 1 == LEAP)
    (like,) = side
    for leap in range(LEAP):
        last = leap + 1 == LEAP
        if leap == 0:
            state = {"q": now["q"], "q0": start, "g0": g0, "mom": mom1, "keep": keep0}
            now = margins_kernel("turn", held, g, h, state)
            position, gap = now["pos"], now["gap"]
        elif not last:
            now = margins_kernel("mid", held, g, h, {"q": now["q"], "p": now["p"]})
        else:
            state = {"q": now["q"], "p": now["p"], "pos": position, "gap": gap, "keep": keep1}
            now = margins_kernel("last", held, g, h, state)
            final_position = assemble(now["pos"], across(now["pos"]))
            sign, final_position = lax.optimization_barrier((sign, final_position))
            signs = (sign, signs[1])
        g, residual, side = gradient(paired(now["margins"]), residual, last, like if last else None)
    distances, likes = side
    momentum = finish_kernel(g, h, now["p"], now["q"])
    return (final_position, assemble(momentum, across(momentum)), likes, distances)


def solution(mesh):
    return jax.shard_map(
        on_device,
        mesh=mesh,
        in_specs=(
            P("rows", "feat"),
            P("rows"),
            P(None, "feat"),
            P(None, None, "feat"),
            P(),
            P(),
            P(),
        ),
        out_specs=(P(None, "feat"), P(None, "feat"), P(), P()),
        check_vma=False,
    )
```

```python
import jax
import jax.numpy as jnp
from jax import lax
from jax.experimental import pallas as pl
from jax.experimental.pallas import tpu as pltpu
from jax.sharding import PartitionSpec as P


FEATURES = 65536
TRANS = 2
LEAP = 5
PAIRS = 8
CHAINS = 16
EXTRA = 128
CHUNKS = 4
GROUP = 4
WIDE = 8
AHEAD = 3

F32 = jnp.float32
BF16 = jnp.bfloat16
VMEM = pl.BlockSpec(memory_space=pltpu.VMEM)
HBM = pl.BlockSpec(memory_space=pltpu.HBM)
SMEM = pl.BlockSpec(memory_space=pltpu.SMEM)
CROSS = (((1,), (1,)), ((), ()))


def limit(mib):
    return pltpu.CompilerParams(vmem_limit_bytes=mib * 1024 * 1024)


def call(body, ins, outs, scratch=(), flops=0, mib=6):
    return pl.pallas_call(
        body,
        in_specs=[spec for _, spec in ins],
        out_specs=[VMEM] * len(outs),
        out_shape=[jax.ShapeDtypeStruct(*o) for o in outs],
        scratch_shapes=list(scratch),
        compiler_params=limit(mib),
        cost_estimate=pl.CostEstimate(flops=flops, bytes_accessed=flops // 16, transcendentals=0),
    )(*[a for a, _ in ins])


def vmem(*arrays):
    return [(a, VMEM) for a in arrays]


def prepare(design, start):
    rows, width = design.shape
    half = width // 2
    step = half // CHUNKS

    def body(start_ref, design_ref, margins_ref, own_ref, away_ref, q_ref, far_ref, sems):
        core = lax.rem(lax.axis_index("rows"), 2)
        near = core * half
        far = (1 - core) * half
        count = [0]

        def fetch(source, target):
            copy = pltpu.make_async_copy(source, target, sems.at[count[0]])
            count[0] += 1
            copy.start()
            return copy

        def cols(offset, size):
            return pl.ds(pl.multiple_of(offset, step), size)

        first = [
            fetch(start_ref.at[:, cols(far, half)], far_ref),
            fetch(start_ref.at[:, cols(near, half)], q_ref),
        ]
        pieces = []
        for offset, target, coefs in ((far, away_ref, far_ref), (near, own_ref, q_ref)):
            for i in range(CHUNKS):
                here = slice(i * step, (i + 1) * step)
                source = design_ref.at[:, cols(offset + i * step, step)]
                pieces.append((source, target.at[:, pl.ds(i * step, step)], target, coefs, here))
        flying = [fetch(*piece[:2]) for piece in pieces[:AHEAD]]
        for copy in first:
            copy.wait()
        total = jnp.zeros((CHAINS, rows), F32)
        for i, (_, _, target, coefs, here) in enumerate(pieces):
            flying[i].wait()
            if i + AHEAD < len(pieces):
                flying.append(fetch(*pieces[i + AHEAD][:2]))
            total = total + lax.dot_general(
                coefs[:, here].astype(BF16), target[:, here], CROSS, preferred_element_type=F32
            )
        margins_ref[...] = total

    piece = ((rows, half), design.dtype)
    return call(
        body,
        [(start, HBM), (design, HBM)],
        [((CHAINS, rows), F32), piece, piece, ((CHAINS, half), F32)],
        [pltpu.VMEM((CHAINS, half), F32), pltpu.SemaphoreType.DMA((2 + 2 * CHUNKS,))],
        2 * CHAINS * rows * width,
        38,
    )


def draw(labels, momenta, lag_offsets, accept_bits, step_sizes):
    rows = labels.shape[0]
    slots, width = momenta.shape[1:]
    half = width // 2

    def body(lag_ref, accept_ref, steps_ref, label_ref, bank_ref, *refs):
        mom0_ref, mom1_ref, h_ref, keep0_ref, keep1_ref, sign_ref, draws_ref, sem = refs
        core = lax.rem(lax.axis_index("rows"), 2)
        cols = pl.ds(pl.multiple_of(core * half, half), half)
        copy = pltpu.make_async_copy(bank_ref.at[:, :, cols], draws_ref, sem)
        copy.start()
        row = lax.broadcasted_iota(jnp.int32, (CHAINS, EXTRA), 0)
        h = jnp.zeros((CHAINS, EXTRA), F32)
        for k in range(PAIRS):
            h = jnp.where(row // 2 == k, steps_ref[k], h)
        h_ref[...] = h
        for s, keep_ref in enumerate((keep0_ref, keep1_ref)):
            keep = jnp.zeros((CHAINS, EXTRA), F32)
            for k in range(CHAINS):
                keep = jnp.where(row == k, accept_ref[s, k].astype(F32), keep)
            keep_ref[...] = keep
        sign_ref[...] = jnp.broadcast_to(label_ref[...].astype(F32), (8, rows))
        copy.wait()
        for s, out_ref in enumerate((mom0_ref, mom1_ref)):
            for k in range(PAIRS):
                out_ref[2 * k : 2 * k + 1] = draws_ref[k, pl.ds(s + lag_ref[k], 1)]
                out_ref[2 * k + 1 : 2 * k + 2] = draws_ref[k, s : s + 1]

    small = ((CHAINS, EXTRA), F32)
    state = ((CHAINS, half), F32)
    return call(
        body,
        [
            (lag_offsets, SMEM),
            (accept_bits, SMEM),
            (step_sizes, SMEM),
            (labels[None, :], VMEM),
            (momenta, HBM),
        ],
        [state, state, small, small, small, ((8, rows), F32)],
        [pltpu.VMEM((PAIRS, slots, half), F32), pltpu.SemaphoreType.DMA],
        0,
        8,
    )


def flip(piece):
    rows, width = piece.shape
    step = 512

    def body(piece_ref, out_ref):
        def one(i, carry):
            cols = pl.ds(pl.multiple_of(i * step, step), step)
            out_ref[cols] = piece_ref[:, cols].T
            return carry

        lax.fori_loop(0, width // step, one, 0)

    return call(body, vmem(piece), [((width, rows), piece.dtype)])[0]


def pair_start(mine, other):
    rows = mine.shape[1]

    def body(mine_ref, other_ref, margins_ref):
        margins_ref[:, :rows] = mine_ref[...]
        margins_ref[:, rows:] = other_ref[...]

    return call(body, vmem(mine, other), [((CHAINS, 2 * rows), F32)])[0]


def pair_sum(mine, other, rows):
    def body(mine_ref, other_ref, out_ref):
        out_ref[:, :rows] = mine_ref[:, :rows] + other_ref[:, rows : 2 * rows]
        out_ref[:, rows : 2 * rows] = mine_ref[:, rows : 2 * rows] + other_ref[:, :rows]
        if mine.shape[1] > 2 * rows:
            out_ref[:, 2 * rows :] = mine_ref[:, 2 * rows :] + other_ref[:, 2 * rows :]

    return call(body, vmem(mine, other), [(mine.shape, F32)])[0]


def assemble(mine, other):
    half = mine.shape[1]

    def body(mine_ref, other_ref, out_ref, sems):
        core = lax.rem(lax.axis_index("rows"), 2)
        copies = []
        for i, (ref, at) in enumerate(((mine_ref, core), (other_ref, 1 - core))):
            cols = pl.ds(pl.multiple_of(at * half, half), half)
            copies.append(pltpu.make_async_copy(ref, out_ref.at[:, cols], sems.at[i]))
            copies[-1].start()
        for copy in copies:
            copy.wait()

    return pl.pallas_call(
        body,
        in_specs=[VMEM, VMEM],
        out_specs=HBM,
        out_shape=jax.ShapeDtypeStruct((CHAINS, 2 * half), F32),
        scratch_shapes=[pltpu.SemaphoreType.DMA((2,))],
        compiler_params=limit(6),
        name="assemble",
    )(mine, other)


def square_gap(position):
    gap = position - pltpu.roll(position, CHAINS - 1, 0)
    return jnp.sum(gap * gap, axis=1, keepdims=True)


def margins_kernel(mode, flipped, arrived, h, state):
    width, rows = flipped[0].shape
    blocks, _, block = arrived.shape
    names = list(state)
    wide = ((CHAINS, width), F32)
    outs = {"margins": ((CHAINS, 2 * rows + (EXTRA if mode == "last" else 0)), F32), "q": wide, "p": wide}
    if mode == "turn":
        outs["pos"] = wide
        outs["gap"] = ((CHAINS, EXTRA), F32)
    if mode == "last":
        outs["pos"] = wide

    def body(own_ref, other_ref, arrived_ref, h_ref, *refs):
        ins = dict(zip(names, refs))
        out = dict(zip(outs, refs[len(names) :]))
        h_col = h_ref[...]
        h_wide = jnp.broadcast_to(h_col[:, :1], (CHAINS, block))
        if mode in ("turn", "last"):
            keep = jnp.broadcast_to(ins["keep"][:, :1], (CHAINS, block)) != 0.0

        def one(b, cols, gap):
            g = arrived_ref[b].astype(F32)
            q = ins["q"][:, cols]
            if mode == "first":
                p = ins["mom"][:, cols] + 0.5 * h_wide * (g - q)
            elif mode == "turn":
                q0 = ins["q0"][:, cols]
                pos = jnp.where(keep, q, q0)
                gradient = jnp.where(keep, g - q, ins["g0"][b].astype(F32) - q0)
                p = ins["mom"][:, cols] + 0.5 * h_wide * gradient
                q = pos
                out["pos"][:, cols] = pos
                gap = gap + square_gap(pos)
            else:
                p = ins["p"][:, cols] + h_wide * (g - q)
            q = q + h_wide * p
            out["p"][:, cols] = p
            out["q"][:, cols] = q
            if mode == "last":
                pos = jnp.where(keep, q, ins["pos"][:, cols])
                out["pos"][:, cols] = pos
                gap = gap + square_gap(pos)
            return q.astype(BF16), gap

        def group(i, carry):
            own, other, gap = carry
            rounded = []
            for j in range(GROUP):
                b = i * GROUP + j
                part, gap = one(b, pl.ds(pl.multiple_of(b * block, block), block), gap)
                rounded.append(part)
            rounded = jnp.concatenate(rounded, axis=1)
            cols = pl.ds(pl.multiple_of(i * (GROUP * block), GROUP * block), GROUP * block)
            own = own + jnp.dot(rounded, own_ref[cols], preferred_element_type=F32)
            other = other + jnp.dot(rounded, other_ref[cols], preferred_element_type=F32)
            return own, other, gap

        zero = jnp.zeros((CHAINS, rows), F32)
        *total, gap = lax.fori_loop(
            0, blocks // GROUP, group, (zero, zero, jnp.zeros((CHAINS, 1), F32))
        )
        if mode == "turn":
            out["gap"][...] = jnp.broadcast_to(gap, (CHAINS, EXTRA))
        if mode == "last":
            lanes = lax.broadcasted_iota(jnp.int32, (CHAINS, EXTRA), 1)
            out["margins"][:, 2 * rows :] = jnp.where(lanes == 0, ins["gap"][...], gap)
        out["margins"][:, :rows] = total[0]
        out["margins"][:, rows : 2 * rows] = total[1]

    result = call(
        body,
        vmem(*flipped, arrived, h, *state.values()),
        list(outs.values()),
        flops=4 * CHAINS * rows * width,
    )
    return dict(zip(outs, result))


def split3(column, first_lane):
    lanes = lax.broadcasted_iota(jnp.int32, (CHAINS, EXTRA), 1) - first_lane
    high = column.astype(BF16).astype(F32)
    middle = (column - high).astype(BF16).astype(F32)
    low = column - high - middle
    out = jnp.where(lanes == 0, high, jnp.zeros((CHAINS, EXTRA), F32))
    out = jnp.where(lanes == 1, middle, out)
    return jnp.where(lanes == 2, low, out)


def terms_kernel(partials, signs, held, blocks, likes, earlier):
    rows, width = held[0].shape
    block = width // blocks
    extended = earlier is not None

    def body(*refs):
        own, one, two, three, mine_ref, theirs_ref, near_ref, far_ref = refs[:8]
        rest = list(refs[8:])
        earlier_ref = rest.pop(0) if extended else None
        out_ref = rest.pop(0)
        total = (own[...] + two[...]) + (one[...] + three[...])
        sign = jnp.concatenate([mine_ref[:1], theirs_ref[:1]], axis=1)
        signed = sign * total[:, : 2 * rows]
        weights = (sign * jax.nn.sigmoid(-signed)).astype(BF16)
        if likes:
            terms = jnp.minimum(signed, 0.0) - jnp.log1p(jnp.exp(-jnp.abs(signed)))
            like = jnp.sum(terms, axis=1, keepdims=True)
            if extended:
                side = split3(earlier_ref[...][:, :1], 0) + split3(like, 3)
                side = side.astype(BF16)
                for b in range(blocks):
                    out_ref[b, :, block:] = side
                squares = total[:, 2 * rows :].T[:2]
                chain = lax.broadcasted_iota(jnp.int32, (CHAINS, PAIRS), 0)
                pair = lax.broadcasted_iota(jnp.int32, (CHAINS, PAIRS), 1)
                leaders = (chain == 2 * pair).astype(F32)
                picked = jnp.dot(
                    squares, leaders, precision=lax.Precision.HIGHEST, preferred_element_type=F32
                )
                rest[0][...] = jnp.sqrt(picked / FEATURES + 1e-06)
            else:
                rest[0][...] = jnp.broadcast_to(like, (CHAINS, EXTRA))

        def group(i, carry):
            for j in range(0, WIDE, GROUP):
                at = i * WIDE + j
                cols = pl.ds(pl.multiple_of(at * block, GROUP * block), GROUP * block)
                terms = jnp.dot(weights[:, :rows], near_ref[:, cols], preferred_element_type=F32)
                far = jnp.dot(weights[:, rows:], far_ref[:, cols], preferred_element_type=F32)
                terms = (terms + far).astype(BF16)
                for b in range(GROUP):
                    out_ref[at + b, :, :block] = terms[:, b * block : (b + 1) * block]
            return carry

        lax.fori_loop(0, blocks // WIDE, group, 0)

    outs = [((blocks, CHAINS, block + (EXTRA if extended else 0)), BF16)]
    if likes:
        outs.append(((TRANS, PAIRS) if extended else (CHAINS, EXTRA), F32))
    return call(
        body,
        vmem(*partials, *signs, *held, *([earlier] if extended else [])),
        outs,
        flops=4 * CHAINS * rows * width,
    )


def sum_kernel(arrived, residual, block, observations):
    blocks = arrived.shape[0]
    carried = residual is not None

    def body(*refs):
        arrived_ref = refs[0]
        send_ref, residual_ref = refs[2 if carried else 1 :][:2]
        parts = [arrived_ref[b, :, :block].astype(F32) for b in range(blocks)]
        while len(parts) > 1:
            parts = [parts[i] + parts[i + 1] for i in range(0, len(parts), 2)]
        exact = parts[0] + refs[1][...] if carried else parts[0]
        send = exact.astype(BF16)
        residual_ref[...] = exact - send.astype(F32)
        for b in range(blocks):
            send_ref[b] = send
        if observations:
            side = jnp.zeros((CHAINS, EXTRA), F32)
            for b in range(blocks):
                side = side + arrived_ref[b, :, block:].astype(F32)
            side = side.T
            for s in range(TRANS):
                like = (side[3 * s : 3 * s + 1] + side[3 * s + 1 : 3 * s + 2]) + side[3 * s + 2 : 3 * s + 3]
                refs[-1][s : s + 1] = like / observations

    outs = [((blocks, CHAINS, block), BF16), ((CHAINS, block), F32)]
    if observations:
        outs.append(((TRANS, CHAINS), F32))
    return call(body, vmem(arrived, *([residual] if carried else [])), outs)


def finish_kernel(arrived, h, p, q):
    blocks, _, block = arrived.shape

    def body(arrived_ref, h_ref, p_ref, q_ref, out_ref):
        half = 0.5 * jnp.broadcast_to(h_ref[...][:, :1], (CHAINS, block))
        for b in range(blocks):
            cols = slice(b * block, (b + 1) * block)
            out_ref[:, cols] = p_ref[:, cols] + half * (arrived_ref[b].astype(F32) - q_ref[:, cols])

    return call(body, vmem(arrived, h, p, q), [((CHAINS, blocks * block), F32)])[0]


def on_device(design, labels, start_position, momenta, lag_offsets, accept_bits, step_sizes):
    rows, _ = design.shape
    devices = lax.axis_size("rows")
    ring = lax.axis_size("feat")
    blocks = devices // 2
    chips = [[2 * k + core for k in range(blocks)] for core in range(2)]
    swap = [(i, i ^ 1) for i in range(devices)]

    def exchange(blocked):
        return lax.all_to_all(blocked, "rows", 0, 0, axis_index_groups=chips)

    def across(value):
        return lax.ppermute(value, "rows", swap)

    def around(margins):
        moved = {}
        for k in (2, 1, 3):
            pairs = [(i, (i + k) % ring) for i in range(ring)]
            moved[k] = lax.ppermute(margins, "feat", pairs)
        return [margins, moved[1], moved[2], moved[3]]

    def gradient(margins, residual, likes=False, earlier=None, beside=None):
        last = earlier is not None
        out, *side = terms_kernel(around(margins), signs, held, blocks, likes, earlier)
        if beside is not None:
            out, beside = lax.optimization_barrier((out, beside))
        block = out.shape[2] - (EXTRA if last else 0)
        send, residual, *totals = sum_kernel(
            exchange(out), residual, block, rows * devices if last else 0
        )
        return exchange(send), residual, side + totals + ([] if beside is None else [beside])

    def paired(margins):
        return pair_sum(margins, across(margins), rows)

    margins, own, away, start = prepare(design, start_position)
    swapped = across(margins)
    away, swapped = lax.optimization_barrier((away, swapped))
    margins = pair_start(margins, swapped)
    held = (own, across(away))
    mom0, mom1, h, keep0, keep1, sign = draw(labels, momenta, lag_offsets, accept_bits, step_sizes)
    sign, own_flipped = lax.optimization_barrier((sign, flip(own)))
    signs = (sign, across(sign))
    g0, residual, (far_flipped,) = gradient(margins, None, beside=flip(held[1]))
    flipped = (own_flipped, far_flipped)
    g = g0
    now = {"q": start}
    for leap in range(LEAP):
        if leap == 0:
            now = margins_kernel("first", flipped, g, h, {"q": start, "mom": mom0})
        else:
            now = margins_kernel("mid", flipped, g, h, {"q": now["q"], "p": now["p"]})
        g, residual, side = gradient(paired(now["margins"]), residual, likes=leap + 1 == LEAP)
    (like,) = side
    for leap in range(LEAP):
        last = leap + 1 == LEAP
        if leap == 0:
            state = {"q": now["q"], "q0": start, "g0": g0, "mom": mom1, "keep": keep0}
            now = margins_kernel("turn", flipped, g, h, state)
            position, gap = now["pos"], now["gap"]
        elif not last:
            now = margins_kernel("mid", flipped, g, h, {"q": now["q"], "p": now["p"]})
        else:
            state = {"q": now["q"], "p": now["p"], "pos": position, "gap": gap, "keep": keep1}
            now = margins_kernel("last", flipped, g, h, state)
            final_position = assemble(now["pos"], across(now["pos"]))
            sign, final_position = lax.optimization_barrier((sign, final_position))
            signs = (sign, signs[1])
        g, residual, side = gradient(paired(now["margins"]), residual, last, like if last else None)
    distances, likes = side
    momentum = finish_kernel(g, h, now["p"], now["q"])
    return (final_position, assemble(momentum, across(momentum)), likes, distances)


def solution(mesh):
    return jax.shard_map(
        on_device,
        mesh=mesh,
        in_specs=(
            P("rows", "feat"),
            P("rows"),
            P(None, "feat"),
            P(None, None, "feat"),
            P(),
            P(),
            P(),
        ),
        out_specs=(P(None, "feat"), P(None, "feat"), P(), P()),
        check_vma=False,
    )
```

```python
import jax
import jax.numpy as jnp
from jax import lax
from jax.experimental import pallas as pl
from jax.experimental.pallas import tpu as pltpu
from jax.sharding import PartitionSpec as P


FEATURES = 65536
TRANS = 2
LEAP = 5
PAIRS = 8
CHAINS = 16
EXTRA = 128
CHUNKS = 4
GROUP = 4
WIDE = 8
DEEP = 8
LOAD = 44

F32 = jnp.float32
BF16 = jnp.bfloat16
VMEM = pl.BlockSpec(memory_space=pltpu.VMEM)
HBM = pl.BlockSpec(memory_space=pltpu.HBM)
SMEM = pl.BlockSpec(memory_space=pltpu.SMEM)
CROSS = (((1,), (1,)), ((), ()))


def limit(mib):
    return pltpu.CompilerParams(vmem_limit_bytes=mib * 1024 * 1024)


def call(body, ins, outs, scratch=(), flops=0, mib=6):
    return pl.pallas_call(
        body,
        in_specs=[spec for _, spec in ins],
        out_specs=[VMEM] * len(outs),
        out_shape=[jax.ShapeDtypeStruct(*o) for o in outs],
        scratch_shapes=list(scratch),
        compiler_params=limit(mib),
        cost_estimate=pl.CostEstimate(flops=flops, bytes_accessed=flops // 16, transcendentals=0),
    )(*[a for a, _ in ins])


def vmem(*arrays):
    return [(a, VMEM) for a in arrays]


def load(design):
    rows, width = design.shape
    half = width // 2

    def body(design_ref, own_ref, away_ref, sems):
        core = lax.rem(lax.axis_index("rows"), 2)
        copies = []
        for n, (side, target) in enumerate(((1 - core, away_ref), (core, own_ref))):
            source = design_ref.at[:, pl.ds(pl.multiple_of(side * half, half), half)]
            copies.append(pltpu.make_async_copy(source, target, sems.at[n]))
            copies[n].start()
        for copy in copies:
            copy.wait()

    piece = ((rows, half), design.dtype)
    ins = [(design, HBM)]
    return call(body, ins, [piece, piece], [pltpu.SemaphoreType.DMA((2,))], 0, LOAD)


def start_margins(own, away, start):
    rows, half = own.shape
    step = half // CHUNKS

    def body(own_ref, away_ref, start_ref, margins_ref, q_ref):
        core = lax.rem(lax.axis_index("rows"), 2)

        def one(i, total):
            here = pl.ds(pl.multiple_of(i * step, step), step)
            near = start_ref[:, pl.ds(pl.multiple_of(core * half + i * step, step), step)]
            far = start_ref[:, pl.ds(pl.multiple_of((1 - core) * half + i * step, step), step)]
            q_ref[:, here] = near
            for value, ref in ((near, own_ref), (far, away_ref)):
                total = total + lax.dot_general(
                    value.astype(BF16), ref[:, here], CROSS, preferred_element_type=F32
                )
            return total

        margins_ref[...] = lax.fori_loop(0, CHUNKS, one, jnp.zeros((CHAINS, rows), F32))

    outs = [((CHAINS, rows), F32), ((CHAINS, half), F32)]
    flops = 4 * CHAINS * rows * half
    return call(body, vmem(own, away, start), outs, flops=flops)


def total_of(own, one, two, three):
    return (own + two) + (one + three)


def ring_sum(partials):
    def body(own, one, two, three, out_ref):
        out_ref[...] = total_of(own[...], one[...], two[...], three[...])

    return call(body, vmem(*partials), [(partials[0].shape, F32)])[0]


def draw(labels, momenta, lag_offsets, accept_bits, step_sizes):
    rows = labels.shape[0]
    slots, width = momenta.shape[1:]
    half = width // 2

    def body(lag_ref, accept_ref, steps_ref, label_ref, bank_ref, *refs):
        mom0_ref, mom1_ref, h_ref, keep0_ref, keep1_ref, sign_ref, draws_ref, sem = refs
        core = lax.rem(lax.axis_index("rows"), 2)
        cols = pl.ds(pl.multiple_of(core * half, half), half)
        copy = pltpu.make_async_copy(bank_ref.at[:, :, cols], draws_ref, sem)
        copy.start()
        row = lax.broadcasted_iota(jnp.int32, (CHAINS, EXTRA), 0)
        h = jnp.zeros((CHAINS, EXTRA), F32)
        for k in range(PAIRS):
            h = jnp.where(row // 2 == k, steps_ref[k], h)
        h_ref[...] = h
        for s, keep_ref in enumerate((keep0_ref, keep1_ref)):
            keep = jnp.zeros((CHAINS, EXTRA), F32)
            for k in range(CHAINS):
                keep = jnp.where(row == k, accept_ref[s, k].astype(F32), keep)
            keep_ref[...] = keep
        sign_ref[...] = jnp.broadcast_to(label_ref[...].astype(F32), (8, rows))
        copy.wait()

        def pick(i, carry):
            here = pl.ds(pl.multiple_of(i * (half // 8), half // 8), half // 8)
            for s, out_ref in enumerate((mom0_ref, mom1_ref)):
                for k in range(PAIRS):
                    out_ref[2 * k : 2 * k + 1, here] = draws_ref[k, pl.ds(s + lag_ref[k], 1), here]
                    out_ref[2 * k + 1 : 2 * k + 2, here] = draws_ref[k, s : s + 1, here]
            return carry

        lax.fori_loop(0, 8, pick, 0)

    small = ((CHAINS, EXTRA), F32)
    state = ((CHAINS, half), F32)
    return call(
        body,
        [
            (lag_offsets, SMEM),
            (accept_bits, SMEM),
            (step_sizes, SMEM),
            (labels[None, :], VMEM),
            (momenta, HBM),
        ],
        [state, state, small, small, small, ((8, rows), F32)],
        [pltpu.VMEM((PAIRS, slots, half), F32), pltpu.SemaphoreType.DMA],
        0,
        8,
    )


def flip(piece):
    rows, width = piece.shape
    step = 512

    def body(piece_ref, out_ref):
        def one(i, carry):
            cols = pl.ds(pl.multiple_of(i * step, step), step)
            out_ref[cols] = piece_ref[:, cols].T
            return carry

        lax.fori_loop(0, width // step, one, 0)

    return call(body, vmem(piece), [((width, rows), piece.dtype)])[0]


def pair_start(mine, other):
    rows = mine.shape[1]

    def body(mine_ref, other_ref, margins_ref):
        margins_ref[:, :rows] = mine_ref[...]
        margins_ref[:, rows:] = other_ref[...]

    return call(body, vmem(mine, other), [((CHAINS, 2 * rows), F32)])[0]


def pair_sum(mine, other, rows):
    def body(mine_ref, other_ref, out_ref):
        out_ref[:, :rows] = mine_ref[:, :rows] + other_ref[:, rows : 2 * rows]
        out_ref[:, rows : 2 * rows] = mine_ref[:, rows : 2 * rows] + other_ref[:, :rows]
        if mine.shape[1] > 2 * rows:
            out_ref[:, 2 * rows :] = mine_ref[:, 2 * rows :] + other_ref[:, 2 * rows :]

    return call(body, vmem(mine, other), [(mine.shape, F32)])[0]


def assemble(mine, other):
    half = mine.shape[1]

    def body(mine_ref, other_ref, out_ref, sems):
        core = lax.rem(lax.axis_index("rows"), 2)
        copies = []
        for i, (ref, at) in enumerate(((mine_ref, core), (other_ref, 1 - core))):
            cols = pl.ds(pl.multiple_of(at * half, half), half)
            copies.append(pltpu.make_async_copy(ref, out_ref.at[:, cols], sems.at[i]))
            copies[-1].start()
        for copy in copies:
            copy.wait()

    return pl.pallas_call(
        body,
        in_specs=[VMEM, VMEM],
        out_specs=HBM,
        out_shape=jax.ShapeDtypeStruct((CHAINS, 2 * half), F32),
        scratch_shapes=[pltpu.SemaphoreType.DMA((2,))],
        compiler_params=limit(6),
        name="assemble",
    )(mine, other)


def square_gap(position):
    gap = position - pltpu.roll(position, CHAINS - 1, 0)
    return jnp.sum(gap * gap, axis=1, keepdims=True)


def margins_kernel(mode, pieces, arrived, h, state):
    flipped = pieces[0].shape[0] > pieces[0].shape[1]
    rows = min(pieces[0].shape)
    width = max(pieces[0].shape)
    blocks, _, block = arrived.shape
    names = list(state)
    wide = ((CHAINS, width), F32)
    outs = {"margins": ((CHAINS, 2 * rows + (EXTRA if mode == "last" else 0)), F32), "q": wide, "p": wide}
    if mode == "turn":
        outs["pos"] = wide
        outs["gap"] = ((CHAINS, EXTRA), F32)
    if mode == "last":
        outs["pos"] = wide

    def body(own_ref, other_ref, arrived_ref, h_ref, *refs):
        ins = dict(zip(names, refs))
        out = dict(zip(outs, refs[len(names) :]))
        h_col = h_ref[...]
        h_wide = jnp.broadcast_to(h_col[:, :1], (CHAINS, block))
        if mode in ("turn", "last"):
            keep = jnp.broadcast_to(ins["keep"][:, :1], (CHAINS, block)) != 0.0

        def one(b, cols, gap):
            g = arrived_ref[b].astype(F32)
            q = ins["q"][:, cols]
            if mode == "first":
                p = ins["mom"][:, cols] + 0.5 * h_wide * (g - q)
            elif mode == "turn":
                q0 = ins["q0"][:, cols]
                pos = jnp.where(keep, q, q0)
                gradient = jnp.where(keep, g - q, ins["g0"][b].astype(F32) - q0)
                p = ins["mom"][:, cols] + 0.5 * h_wide * gradient
                q = pos
                out["pos"][:, cols] = pos
                gap = gap + square_gap(pos)
            else:
                p = ins["p"][:, cols] + h_wide * (g - q)
            q = q + h_wide * p
            out["p"][:, cols] = p
            out["q"][:, cols] = q
            if mode == "last":
                pos = jnp.where(keep, q, ins["pos"][:, cols])
                out["pos"][:, cols] = pos
                gap = gap + square_gap(pos)
            return q.astype(BF16), gap

        def group(i, carry):
            own, other, gap = carry
            rounded = []
            for j in range(DEEP):
                b = i * DEEP + j
                part, gap = one(b, pl.ds(pl.multiple_of(b * block, block), block), gap)
                rounded.append(part)
            rounded = jnp.concatenate(rounded, axis=1)
            cols = pl.ds(pl.multiple_of(i * (DEEP * block), DEEP * block), DEEP * block)
            if flipped:
                own = own + jnp.dot(rounded, own_ref[cols], preferred_element_type=F32)
                other = other + jnp.dot(rounded, other_ref[cols], preferred_element_type=F32)
            else:
                own = own + lax.dot_general(
                    rounded, own_ref[:, cols], CROSS, preferred_element_type=F32
                )
                other = other + lax.dot_general(
                    rounded, other_ref[:, cols], CROSS, preferred_element_type=F32
                )
            return own, other, gap

        zero = jnp.zeros((CHAINS, rows), F32)
        *total, gap = lax.fori_loop(
            0, blocks // DEEP, group, (zero, zero, jnp.zeros((CHAINS, 1), F32))
        )
        if mode == "turn":
            out["gap"][...] = jnp.broadcast_to(gap, (CHAINS, EXTRA))
        if mode == "last":
            lanes = lax.broadcasted_iota(jnp.int32, (CHAINS, EXTRA), 1)
            out["margins"][:, 2 * rows :] = jnp.where(lanes == 0, ins["gap"][...], gap)
        out["margins"][:, :rows] = total[0]
        out["margins"][:, rows : 2 * rows] = total[1]

    result = call(
        body,
        vmem(*pieces, arrived, h, *state.values()),
        list(outs.values()),
        flops=4 * CHAINS * rows * width,
    )
    return dict(zip(outs, result))


def split3(column, first_lane):
    lanes = lax.broadcasted_iota(jnp.int32, (CHAINS, EXTRA), 1) - first_lane
    high = column.astype(BF16).astype(F32)
    middle = (column - high).astype(BF16).astype(F32)
    low = column - high - middle
    out = jnp.where(lanes == 0, high, jnp.zeros((CHAINS, EXTRA), F32))
    out = jnp.where(lanes == 1, middle, out)
    return jnp.where(lanes == 2, low, out)


def terms_kernel(partials, signs, held, blocks, likes, earlier):
    rows, width = held[0].shape
    block = width // blocks
    extended = earlier is not None

    def body(*refs):
        sums = [ref[...] for ref in refs[: len(partials)]]
        mine_ref, theirs_ref, near_ref, far_ref = refs[len(partials) : len(partials) + 4]
        rest = list(refs[len(partials) + 4 :])
        earlier_ref = rest.pop(0) if extended else None
        out_ref = rest.pop(0)
        total = total_of(*sums) if len(sums) > 1 else sums[0]
        sign = jnp.concatenate([mine_ref[:1], theirs_ref[:1]], axis=1)
        signed = sign * total[:, : 2 * rows]
        weights = (sign * jax.nn.sigmoid(-signed)).astype(BF16)
        if likes:
            terms = jnp.minimum(signed, 0.0) - jnp.log1p(jnp.exp(-jnp.abs(signed)))
            like = jnp.sum(terms, axis=1, keepdims=True)
            if extended:
                side = split3(earlier_ref[...][:, :1], 0) + split3(like, 3)
                side = side.astype(BF16)
                for b in range(blocks):
                    out_ref[b, :, block:] = side
                squares = total[:, 2 * rows :].T[:2]
                chain = lax.broadcasted_iota(jnp.int32, (CHAINS, PAIRS), 0)
                pair = lax.broadcasted_iota(jnp.int32, (CHAINS, PAIRS), 1)
                leaders = (chain == 2 * pair).astype(F32)
                picked = jnp.dot(
                    squares, leaders, precision=lax.Precision.HIGHEST, preferred_element_type=F32
                )
                rest[0][...] = jnp.sqrt(picked / FEATURES + 1e-06)
            else:
                rest[0][...] = jnp.broadcast_to(like, (CHAINS, EXTRA))

        def group(i, carry):
            for j in range(0, WIDE, GROUP):
                at = i * WIDE + j
                cols = pl.ds(pl.multiple_of(at * block, GROUP * block), GROUP * block)
                terms = jnp.dot(weights[:, :rows], near_ref[:, cols], preferred_element_type=F32)
                far = jnp.dot(weights[:, rows:], far_ref[:, cols], preferred_element_type=F32)
                terms = (terms + far).astype(BF16)
                for b in range(GROUP):
                    out_ref[at + b, :, :block] = terms[:, b * block : (b + 1) * block]
            return carry

        lax.fori_loop(0, blocks // WIDE, group, 0)

    outs = [((blocks, CHAINS, block + (EXTRA if extended else 0)), BF16)]
    if likes:
        outs.append(((TRANS, PAIRS) if extended else (CHAINS, EXTRA), F32))
    return call(
        body,
        vmem(*partials, *signs, *held, *([earlier] if extended else [])),
        outs,
        flops=4 * CHAINS * rows * width,
    )


def sum_kernel(arrived, residual, block, observations):
    blocks = arrived.shape[0]
    carried = residual is not None

    def body(*refs):
        arrived_ref = refs[0]
        send_ref, residual_ref = refs[2 if carried else 1 :][:2]
        parts = [arrived_ref[b, :, :block].astype(F32) for b in range(blocks)]
        while len(parts) > 1:
            parts = [parts[i] + parts[i + 1] for i in range(0, len(parts), 2)]
        exact = parts[0] + refs[1][...] if carried else parts[0]
        send = exact.astype(BF16)
        residual_ref[...] = exact - send.astype(F32)
        for b in range(blocks):
            send_ref[b] = send
        if observations:
            side = jnp.zeros((CHAINS, EXTRA), F32)
            for b in range(blocks):
                side = side + arrived_ref[b, :, block:].astype(F32)
            side = side.T
            for s in range(TRANS):
                like = (side[3 * s : 3 * s + 1] + side[3 * s + 1 : 3 * s + 2]) + side[3 * s + 2 : 3 * s + 3]
                refs[-1][s : s + 1] = like / observations

    outs = [((blocks, CHAINS, block), BF16), ((CHAINS, block), F32)]
    if observations:
        outs.append(((TRANS, CHAINS), F32))
    return call(body, vmem(arrived, *([residual] if carried else [])), outs)


def finish_kernel(arrived, h, p, q):
    blocks, _, block = arrived.shape

    def body(arrived_ref, h_ref, p_ref, q_ref, out_ref):
        half = 0.5 * jnp.broadcast_to(h_ref[...][:, :1], (CHAINS, block))
        for b in range(blocks):
            cols = slice(b * block, (b + 1) * block)
            out_ref[:, cols] = p_ref[:, cols] + half * (arrived_ref[b].astype(F32) - q_ref[:, cols])

    return call(body, vmem(arrived, h, p, q), [((CHAINS, blocks * block), F32)])[0]


def on_device(design, labels, start_position, momenta, lag_offsets, accept_bits, step_sizes):
    rows, _ = design.shape
    devices = lax.axis_size("rows")
    ring = lax.axis_size("feat")
    blocks = devices // 2
    chips = [[2 * k + core for k in range(blocks)] for core in range(2)]
    swap = [(i, i ^ 1) for i in range(devices)]

    def exchange(blocked):
        return lax.all_to_all(blocked, "rows", 0, 0, axis_index_groups=chips)

    def across(value):
        return lax.ppermute(value, "rows", swap)

    def around(margins):
        moved = {}
        for k in (2, 1, 3):
            pairs = [(i, (i + k) % ring) for i in range(ring)]
            moved[k] = lax.ppermute(margins, "feat", pairs)
        return [margins, moved[1], moved[2], moved[3]]

    def gradient(partials, residual, likes=False, earlier=None, beside=()):
        last = earlier is not None
        out, *side = terms_kernel(partials, signs, held, blocks, likes, earlier)
        out, *beside = lax.optimization_barrier((out, *beside))
        block = out.shape[2] - (EXTRA if last else 0)
        send, residual, *totals = sum_kernel(
            exchange(out), residual, block, rows * devices if last else 0
        )
        return exchange(send), residual, side + totals + beside

    def paired(margins):
        return around(pair_sum(margins, across(margins), rows))

    own, away = load(design)
    held = (own, across(away))
    margins, start = start_margins(own, away, start_position)
    mom0, mom1, h, keep0, keep1, sign = draw(labels, momenta, lag_offsets, accept_bits, step_sizes)
    signs = (sign, across(sign))
    margins = ring_sum(around(margins))
    margins = pair_start(margins, across(margins))
    g0, residual, (mom0, mom1) = gradient([margins], None, beside=(mom0, mom1))
    g = g0
    pieces = held
    flips = []
    now = {"q": start}
    for leap in range(LEAP):
        if leap == 0:
            now = margins_kernel("first", pieces, g, h, {"q": start, "mom": mom0})
        else:
            now = margins_kernel("mid", pieces, g, h, {"q": now["q"], "p": now["p"]})
        partials = paired(now["margins"])
        beside = (flip(held[leap]),) if leap < len(held) else ()
        g, residual, side = gradient(partials, residual, leap + 1 == LEAP, beside=beside)
        if beside:
            flips += side
        if len(flips) == len(held):
            pieces = tuple(flips)
    (like,) = side
    for leap in range(LEAP):
        last = leap + 1 == LEAP
        if leap == 0:
            state = {"q": now["q"], "q0": start, "g0": g0, "mom": mom1, "keep": keep0}
            now = margins_kernel("turn", pieces, g, h, state)
            position, gap = now["pos"], now["gap"]
        elif not last:
            now = margins_kernel("mid", pieces, g, h, {"q": now["q"], "p": now["p"]})
        else:
            state = {"q": now["q"], "p": now["p"], "pos": position, "gap": gap, "keep": keep1}
            now = margins_kernel("last", pieces, g, h, state)
            final_position = assemble(now["pos"], across(now["pos"]))
            sign, final_position = lax.optimization_barrier((sign, final_position))
            signs = (sign, signs[1])
        g, residual, side = gradient(
            paired(now["margins"]), residual, last, like if last else None
        )
    distances, likes = side
    momentum = finish_kernel(g, h, now["p"], now["q"])
    return (final_position, assemble(momentum, across(momentum)), likes, distances)


def solution(mesh):
    return jax.shard_map(
        on_device,
        mesh=mesh,
        in_specs=(
            P("rows", "feat"),
            P("rows"),
            P(None, "feat"),
            P(None, None, "feat"),
            P(),
            P(),
            P(),
        ),
        out_specs=(P(None, "feat"), P(None, "feat"), P(), P()),
        check_vma=False,
    )
```

```python
import jax
import jax.numpy as jnp
from jax import lax
from jax.experimental import pallas as pl
from jax.experimental.pallas import tpu as pltpu
from jax.sharding import PartitionSpec as P


FEATURES = 65536
TRANS = 2
LEAP = 5
PAIRS = 8
CHAINS = 16
EXTRA = 128
CHUNKS = 4
GROUP = 4
WIDE = 8
DEEP = 8
LOAD = 44

F32 = jnp.float32
BF16 = jnp.bfloat16
VMEM = pl.BlockSpec(memory_space=pltpu.VMEM)
HBM = pl.BlockSpec(memory_space=pltpu.HBM)
SMEM = pl.BlockSpec(memory_space=pltpu.SMEM)
CROSS = (((1,), (1,)), ((), ()))


def limit(mib):
    return pltpu.CompilerParams(vmem_limit_bytes=mib * 1024 * 1024)


def call(body, ins, outs, scratch=(), flops=0, mib=6):
    return pl.pallas_call(
        body,
        in_specs=[spec for _, spec in ins],
        out_specs=[VMEM] * len(outs),
        out_shape=[jax.ShapeDtypeStruct(*o) for o in outs],
        scratch_shapes=list(scratch),
        compiler_params=limit(mib),
        cost_estimate=pl.CostEstimate(flops=flops, bytes_accessed=flops // 16, transcendentals=0),
    )(*[a for a, _ in ins])


def vmem(*arrays):
    return [(a, VMEM) for a in arrays]


def load(design):
    rows, width = design.shape
    half = width // 2

    def body(design_ref, own_ref, away_ref, sems):
        core = lax.rem(lax.axis_index("rows"), 2)
        copies = []
        for n, (side, target) in enumerate(((1 - core, away_ref), (core, own_ref))):
            source = design_ref.at[:, pl.ds(pl.multiple_of(side * half, half), half)]
            copies.append(pltpu.make_async_copy(source, target, sems.at[n]))
            copies[n].start()
        for copy in copies:
            copy.wait()

    piece = ((rows, half), design.dtype)
    ins = [(design, HBM)]
    return call(body, ins, [piece, piece], [pltpu.SemaphoreType.DMA((2,))], 0, LOAD)


def start_margins(own, away, start):
    rows, half = own.shape
    step = half // CHUNKS

    def body(own_ref, away_ref, start_ref, margins_ref, q_ref):
        core = lax.rem(lax.axis_index("rows"), 2)

        def one(i, total):
            here = pl.ds(pl.multiple_of(i * step, step), step)
            near = start_ref[:, pl.ds(pl.multiple_of(core * half + i * step, step), step)]
            far = start_ref[:, pl.ds(pl.multiple_of((1 - core) * half + i * step, step), step)]
            q_ref[:, here] = near
            for value, ref in ((near, own_ref), (far, away_ref)):
                total = total + lax.dot_general(
                    value.astype(BF16), ref[:, here], CROSS, preferred_element_type=F32
                )
            return total

        margins_ref[...] = lax.fori_loop(0, CHUNKS, one, jnp.zeros((CHAINS, rows), F32))

    outs = [((CHAINS, rows), F32), ((CHAINS, half), F32)]
    flops = 4 * CHAINS * rows * half
    return call(body, vmem(own, away, start), outs, flops=flops)


def total_of(own, one, two, three):
    return (own + two) + (one + three)


def ring_sum(partials):
    def body(own, one, two, three, out_ref):
        out_ref[...] = total_of(own[...], one[...], two[...], three[...])

    return call(body, vmem(*partials), [(partials[0].shape, F32)])[0]


def draw(labels, momenta, lag_offsets, accept_bits, step_sizes):
    rows = labels.shape[0]
    slots, width = momenta.shape[1:]
    half = width // 2

    def body(lag_ref, accept_ref, steps_ref, label_ref, bank_ref, *refs):
        mom0_ref, mom1_ref, h_ref, keep0_ref, keep1_ref, sign_ref, draws_ref, sem = refs
        core = lax.rem(lax.axis_index("rows"), 2)
        cols = pl.ds(pl.multiple_of(core * half, half), half)
        copy = pltpu.make_async_copy(bank_ref.at[:, :, cols], draws_ref, sem)
        copy.start()
        row = lax.broadcasted_iota(jnp.int32, (CHAINS, EXTRA), 0)
        h = jnp.zeros((CHAINS, EXTRA), F32)
        for k in range(PAIRS):
            h = jnp.where(row // 2 == k, steps_ref[k], h)
        h_ref[...] = h
        for s, keep_ref in enumerate((keep0_ref, keep1_ref)):
            keep = jnp.zeros((CHAINS, EXTRA), F32)
            for k in range(CHAINS):
                keep = jnp.where(row == k, accept_ref[s, k].astype(F32), keep)
            keep_ref[...] = keep
        sign_ref[...] = jnp.broadcast_to(label_ref[...].astype(F32), (8, rows))
        copy.wait()

        def pick(i, carry):
            here = pl.ds(pl.multiple_of(i * (half // 8), half // 8), half // 8)
            for s, out_ref in enumerate((mom0_ref, mom1_ref)):
                for k in range(PAIRS):
                    out_ref[2 * k : 2 * k + 1, here] = draws_ref[k, pl.ds(s + lag_ref[k], 1), here]
                    out_ref[2 * k + 1 : 2 * k + 2, here] = draws_ref[k, s : s + 1, here]
            return carry

        lax.fori_loop(0, 8, pick, 0)

    small = ((CHAINS, EXTRA), F32)
    state = ((CHAINS, half), F32)
    return call(
        body,
        [
            (lag_offsets, SMEM),
            (accept_bits, SMEM),
            (step_sizes, SMEM),
            (labels[None, :], VMEM),
            (momenta, HBM),
        ],
        [state, state, small, small, small, ((8, rows), F32)],
        [pltpu.VMEM((PAIRS, slots, half), F32), pltpu.SemaphoreType.DMA],
        0,
        8,
    )


def flip(piece):
    rows, width = piece.shape
    step = 512

    def body(piece_ref, out_ref):
        def one(i, carry):
            cols = pl.ds(pl.multiple_of(i * step, step), step)
            out_ref[cols] = piece_ref[:, cols].T
            return carry

        lax.fori_loop(0, width // step, one, 0)

    return call(body, vmem(piece), [((width, rows), piece.dtype)])[0]


def pair_start(mine, other):
    rows = mine.shape[1]

    def body(mine_ref, other_ref, margins_ref):
        margins_ref[:, :rows] = mine_ref[...]
        margins_ref[:, rows:] = other_ref[...]

    return call(body, vmem(mine, other), [((CHAINS, 2 * rows), F32)])[0]


def pair_sum(mine, other, rows):
    def body(mine_ref, other_ref, out_ref):
        out_ref[:, :rows] = mine_ref[:, :rows] + other_ref[:, rows : 2 * rows]
        out_ref[:, rows : 2 * rows] = mine_ref[:, rows : 2 * rows] + other_ref[:, :rows]
        if mine.shape[1] > 2 * rows:
            out_ref[:, 2 * rows :] = mine_ref[:, 2 * rows :] + other_ref[:, 2 * rows :]

    return call(body, vmem(mine, other), [(mine.shape, F32)])[0]


def assemble(mine, other):
    half = mine.shape[1]

    def body(mine_ref, other_ref, out_ref, sems):
        core = lax.rem(lax.axis_index("rows"), 2)
        copies = []
        for i, (ref, at) in enumerate(((mine_ref, core), (other_ref, 1 - core))):
            cols = pl.ds(pl.multiple_of(at * half, half), half)
            copies.append(pltpu.make_async_copy(ref, out_ref.at[:, cols], sems.at[i]))
            copies[-1].start()
        for copy in copies:
            copy.wait()

    return pl.pallas_call(
        body,
        in_specs=[VMEM, VMEM],
        out_specs=HBM,
        out_shape=jax.ShapeDtypeStruct((CHAINS, 2 * half), F32),
        scratch_shapes=[pltpu.SemaphoreType.DMA((2,))],
        compiler_params=limit(6),
        name="assemble",
    )(mine, other)


def square_gap(position):
    gap = position - pltpu.roll(position, CHAINS - 1, 0)
    return jnp.sum(gap * gap, axis=1, keepdims=True)


def margins_kernel(mode, pieces, arrived, h, state):
    flipped = pieces[0].shape[0] > pieces[0].shape[1]
    rows = min(pieces[0].shape)
    width = max(pieces[0].shape)
    blocks, _, block = arrived.shape
    names = list(state)
    wide = ((CHAINS, width), F32)
    outs = {"margins": ((CHAINS, 2 * rows + (EXTRA if mode == "last" else 0)), F32), "q": wide, "p": wide}
    if mode == "turn":
        outs["pos"] = wide
        outs["gap"] = ((CHAINS, EXTRA), F32)
    if mode == "last":
        outs = {"margins": outs["margins"], "base": wide, "pos": wide}

    def body(own_ref, other_ref, arrived_ref, h_ref, *refs):
        ins = dict(zip(names, refs))
        out = dict(zip(outs, refs[len(names) :]))
        h_col = h_ref[...]
        h_wide = jnp.broadcast_to(h_col[:, :1], (CHAINS, block))
        if mode in ("turn", "last"):
            keep = jnp.broadcast_to(ins["keep"][:, :1], (CHAINS, block)) != 0.0

        def one(b, cols, gap):
            g = arrived_ref[b].astype(F32)
            q = ins["q"][:, cols]
            if mode == "first":
                p = ins["mom"][:, cols] + 0.5 * h_wide * (g - q)
            elif mode == "turn":
                q0 = ins["q0"][:, cols]
                pos = jnp.where(keep, q, q0)
                gradient = jnp.where(keep, g - q, ins["g0"][b].astype(F32) - q0)
                p = ins["mom"][:, cols] + 0.5 * h_wide * gradient
                q = pos
                out["pos"][:, cols] = pos
                gap = gap + square_gap(pos)
            else:
                p = ins["p"][:, cols] + h_wide * (g - q)
            q = q + h_wide * p
            if mode == "last":
                out["base"][:, cols] = p - 0.5 * h_wide * q
            else:
                out["p"][:, cols] = p
                out["q"][:, cols] = q
            if mode == "last":
                pos = jnp.where(keep, q, ins["pos"][:, cols])
                out["pos"][:, cols] = pos
                gap = gap + square_gap(pos)
            return q.astype(BF16), gap

        def group(i, carry):
            own, other, gap = carry
            rounded = []
            for j in range(DEEP):
                b = i * DEEP + j
                part, gap = one(b, pl.ds(pl.multiple_of(b * block, block), block), gap)
                rounded.append(part)
            rounded = jnp.concatenate(rounded, axis=1)
            cols = pl.ds(pl.multiple_of(i * (DEEP * block), DEEP * block), DEEP * block)
            if flipped:
                own = own + jnp.dot(rounded, own_ref[cols], preferred_element_type=F32)
                other = other + jnp.dot(rounded, other_ref[cols], preferred_element_type=F32)
            else:
                own = own + lax.dot_general(
                    rounded, own_ref[:, cols], CROSS, preferred_element_type=F32
                )
                other = other + lax.dot_general(
                    rounded, other_ref[:, cols], CROSS, preferred_element_type=F32
                )
            return own, other, gap

        zero = jnp.zeros((CHAINS, rows), F32)
        *total, gap = lax.fori_loop(
            0, blocks // DEEP, group, (zero, zero, jnp.zeros((CHAINS, 1), F32))
        )
        if mode == "turn":
            out["gap"][...] = jnp.broadcast_to(gap, (CHAINS, EXTRA))
        if mode == "last":
            lanes = lax.broadcasted_iota(jnp.int32, (CHAINS, EXTRA), 1)
            out["margins"][:, 2 * rows :] = jnp.where(lanes == 0, ins["gap"][...], gap)
        out["margins"][:, :rows] = total[0]
        out["margins"][:, rows : 2 * rows] = total[1]

    result = call(
        body,
        vmem(*pieces, arrived, h, *state.values()),
        list(outs.values()),
        flops=4 * CHAINS * rows * width,
    )
    return dict(zip(outs, result))


def split3(column, first_lane):
    lanes = lax.broadcasted_iota(jnp.int32, (CHAINS, EXTRA), 1) - first_lane
    high = column.astype(BF16).astype(F32)
    middle = (column - high).astype(BF16).astype(F32)
    low = column - high - middle
    out = jnp.where(lanes == 0, high, jnp.zeros((CHAINS, EXTRA), F32))
    out = jnp.where(lanes == 1, middle, out)
    return jnp.where(lanes == 2, low, out)


def terms_kernel(partials, signs, held, blocks, likes, earlier):
    rows, width = held[0].shape
    block = width // blocks
    extended = earlier is not None

    def body(*refs):
        sums = [ref[...] for ref in refs[: len(partials)]]
        mine_ref, theirs_ref, near_ref, far_ref = refs[len(partials) : len(partials) + 4]
        rest = list(refs[len(partials) + 4 :])
        earlier_ref = rest.pop(0) if extended else None
        out_ref = rest.pop(0)
        total = total_of(*sums) if len(sums) > 1 else sums[0]
        sign = jnp.concatenate([mine_ref[:1], theirs_ref[:1]], axis=1)
        signed = sign * total[:, : 2 * rows]
        weights = (sign * jax.nn.sigmoid(-signed)).astype(BF16)
        if likes:
            terms = jnp.minimum(signed, 0.0) - jnp.log1p(jnp.exp(-jnp.abs(signed)))
            like = jnp.sum(terms, axis=1, keepdims=True)
            if extended:
                side = split3(earlier_ref[...][:, :1], 0) + split3(like, 3)
                side = side.astype(BF16)
                for b in range(blocks):
                    out_ref[b, :, block:] = side
                rest[0][...] = total[:, 2 * rows :]
            else:
                rest[0][...] = jnp.broadcast_to(like, (CHAINS, EXTRA))

        def group(i, carry):
            for j in range(0, WIDE, GROUP):
                at = i * WIDE + j
                cols = pl.ds(pl.multiple_of(at * block, GROUP * block), GROUP * block)
                terms = jnp.dot(weights[:, :rows], near_ref[:, cols], preferred_element_type=F32)
                far = jnp.dot(weights[:, rows:], far_ref[:, cols], preferred_element_type=F32)
                terms = (terms + far).astype(BF16)
                for b in range(GROUP):
                    out_ref[at + b, :, :block] = terms[:, b * block : (b + 1) * block]
            return carry

        lax.fori_loop(0, blocks // WIDE, group, 0)

    outs = [((blocks, CHAINS, block + (EXTRA if extended else 0)), BF16)]
    if likes:
        outs.append(((CHAINS, EXTRA), F32))
    return call(
        body,
        vmem(*partials, *signs, *held, *([earlier] if extended else [])),
        outs,
        flops=4 * CHAINS * rows * width,
    )


def sum_kernel(arrived, residual, block, likes):
    blocks = arrived.shape[0]
    carried = residual is not None

    def body(*refs):
        arrived_ref = refs[0]
        send_ref, second_ref = refs[2 if carried else 1 :]
        parts = [arrived_ref[b, :, :block].astype(F32) for b in range(blocks)]
        while len(parts) > 1:
            parts = [parts[i] + parts[i + 1] for i in range(0, len(parts), 2)]
        exact = parts[0] + refs[1][...] if carried else parts[0]
        send = exact.astype(BF16)
        if not likes:
            second_ref[...] = exact - send.astype(F32)
        for b in range(blocks):
            send_ref[b] = send
        if likes:
            side = jnp.zeros((CHAINS, EXTRA), F32)
            for b in range(blocks):
                side = side + arrived_ref[b, :, block:].astype(F32)
            second_ref[...] = side

    outs = [((blocks, CHAINS, block), BF16), ((CHAINS, EXTRA if likes else block), F32)]
    return call(body, vmem(arrived, *([residual] if carried else [])), outs)


def scores(squares, sides, observations):
    def body(square_ref, side_ref, distance_ref, like_ref):
        chain = lax.broadcasted_iota(jnp.int32, (CHAINS, PAIRS), 0)
        pair = lax.broadcasted_iota(jnp.int32, (CHAINS, PAIRS), 1)
        picked = jnp.dot(
            square_ref[...].T[:TRANS],
            (chain == 2 * pair).astype(F32),
            precision=lax.Precision.HIGHEST,
            preferred_element_type=F32,
        )
        distance_ref[...] = jnp.sqrt(picked / FEATURES + 1e-06)
        side = side_ref[...].T
        for s in range(TRANS):
            high, middle, low = (side[3 * s + i : 3 * s + i + 1] for i in range(3))
            like_ref[s : s + 1] = ((high + middle) + low) / observations

    return call(body, vmem(squares, sides), [((TRANS, PAIRS), F32), ((TRANS, CHAINS), F32)])


def finish_kernel(mine, other, half_step, base):
    blocks, _, block = mine.shape
    half = blocks * block

    def body(mine_ref, other_ref, h_ref, mine_base, other_base, out_ref, held_ref, sems):
        core = lax.rem(lax.axis_index("rows"), 2)
        step = 0.5 * jnp.broadcast_to(h_ref[...][:, :1], (CHAINS, block))
        copies = []
        for n, (side, ref, base_ref) in enumerate(
            ((core, mine_ref, mine_base), (1 - core, other_ref, other_base))
        ):

            def one(i, carry):
                for j in range(GROUP):
                    b = i * GROUP + j
                    cols = pl.ds(pl.multiple_of(b * block, block), block)
                    held_ref[n, :, cols] = base_ref[:, cols] + step * ref[b].astype(F32)
                return carry

            lax.fori_loop(0, blocks // GROUP, one, 0)
            target = out_ref.at[:, pl.ds(pl.multiple_of(side * half, half), half)]
            copies.append(pltpu.make_async_copy(held_ref.at[n], target, sems.at[n]))
            copies[n].start()
        for copy in copies:
            copy.wait()

    return pl.pallas_call(
        body,
        in_specs=[VMEM] * 5,
        out_specs=HBM,
        out_shape=jax.ShapeDtypeStruct((CHAINS, 2 * half), F32),
        scratch_shapes=[pltpu.VMEM((2, CHAINS, half), F32), pltpu.SemaphoreType.DMA((2,))],
        compiler_params=limit(6),
        name="finish",
    )(mine, other, half_step, *base)


def on_device(design, labels, start_position, momenta, lag_offsets, accept_bits, step_sizes):
    rows, _ = design.shape
    devices = lax.axis_size("rows")
    ring = lax.axis_size("feat")
    blocks = devices // 2
    chips = [[2 * k + core for k in range(blocks)] for core in range(2)]
    swap = [(i, i ^ 1) for i in range(devices)]

    def exchange(blocked):
        return lax.all_to_all(blocked, "rows", 0, 0, axis_index_groups=chips)

    def across(value):
        return lax.ppermute(value, "rows", swap)

    def around(margins):
        moved = {}
        for k in (2, 1, 3):
            pairs = [(i, (i + k) % ring) for i in range(ring)]
            moved[k] = lax.ppermute(margins, "feat", pairs)
        return [margins, moved[1], moved[2], moved[3]]

    def gradient(partials, residual, likes=False, earlier=None, beside=()):
        last = earlier is not None
        out, *side = terms_kernel(partials, signs, held, blocks, likes, earlier)
        out, *beside = lax.optimization_barrier((out, *beside))
        block = out.shape[2] - (EXTRA if last else 0)
        send, second = sum_kernel(exchange(out), residual, block, last)
        residual, totals = (None, [second]) if last else (second, [])
        return exchange(send), residual, side + totals + beside

    def paired(margins):
        return around(pair_sum(margins, across(margins), rows))

    own, away = load(design)
    held = (own, across(away))
    margins, start = start_margins(own, away, start_position)
    mom0, mom1, h, keep0, keep1, sign = draw(labels, momenta, lag_offsets, accept_bits, step_sizes)
    signs = (sign, across(sign))
    margins = ring_sum(around(margins))
    margins = pair_start(margins, across(margins))
    g0, residual, (mom0, mom1) = gradient([margins], None, beside=(mom0, mom1))
    g = g0
    pieces = held
    flips = []
    now = {"q": start}
    for leap in range(LEAP):
        if leap == 0:
            now = margins_kernel("first", pieces, g, h, {"q": start, "mom": mom0})
        else:
            now = margins_kernel("mid", pieces, g, h, {"q": now["q"], "p": now["p"]})
        partials = paired(now["margins"])
        beside = (flip(held[leap]),) if leap < len(held) else ()
        g, residual, side = gradient(partials, residual, leap + 1 == LEAP, beside=beside)
        if beside:
            flips += side
        if len(flips) == len(held):
            pieces = tuple(flips)
    (like,) = side
    for leap in range(LEAP):
        last = leap + 1 == LEAP
        if leap == 0:
            state = {"q": now["q"], "q0": start, "g0": g0, "mom": mom1, "keep": keep0}
            now = margins_kernel("turn", pieces, g, h, state)
            position, gap = now["pos"], now["gap"]
        elif not last:
            now = margins_kernel("mid", pieces, g, h, {"q": now["q"], "p": now["p"]})
        else:
            state = {"q": now["q"], "p": now["p"], "pos": position, "gap": gap, "keep": keep1}
            now = margins_kernel("last", pieces, g, h, state)
            swapped, position, base = lax.optimization_barrier(
                (across(now["margins"]), now["pos"], now["base"])
            )
            partials = around(pair_sum(now["margins"], swapped, rows))
            final_position = assemble(position, across(position))
            base = (base, across(base))
            sign, final_position, base = lax.optimization_barrier((sign, final_position, base))
            signs = (sign, signs[1])
        if not last:
            partials = paired(now["margins"])
        g, residual, side = gradient(partials, residual, last, like if last else None)
    squares, sides = side
    g, squares, sides = lax.optimization_barrier((g, squares, sides))
    distances, likes = scores(squares, sides, rows * devices)
    momentum = finish_kernel(g, across(g), h, base)
    return (final_position, momentum, likes, distances)


def solution(mesh):
    return jax.shard_map(
        on_device,
        mesh=mesh,
        in_specs=(
            P("rows", "feat"),
            P("rows"),
            P(None, "feat"),
            P(None, None, "feat"),
            P(),
            P(),
            P(),
        ),
        out_specs=(P(None, "feat"), P(None, "feat"), P(), P()),
        check_vma=False,
    )
```

```python
import jax
import jax.numpy as jnp
from jax import lax
from jax.experimental import pallas as pl
from jax.experimental.pallas import tpu as pltpu
from jax.sharding import PartitionSpec as P


FEATURES = 65536
TRANS = 2
LEAP = 5
PAIRS = 8
CHAINS = 16
EXTRA = 128
CHUNKS = 4
GROUP = 4
WIDE = 8
DEEP = 8
LOAD = 44

F32 = jnp.float32
BF16 = jnp.bfloat16
VMEM = pl.BlockSpec(memory_space=pltpu.VMEM)
HBM = pl.BlockSpec(memory_space=pltpu.HBM)
SMEM = pl.BlockSpec(memory_space=pltpu.SMEM)
CROSS = (((1,), (1,)), ((), ()))


def limit(mib):
    return pltpu.CompilerParams(vmem_limit_bytes=mib * 1024 * 1024)


def call(body, ins, outs, scratch=(), flops=0, mib=6):
    return pl.pallas_call(
        body,
        in_specs=[spec for _, spec in ins],
        out_specs=[VMEM] * len(outs),
        out_shape=[jax.ShapeDtypeStruct(*o) for o in outs],
        scratch_shapes=list(scratch),
        compiler_params=limit(mib),
        cost_estimate=pl.CostEstimate(flops=flops, bytes_accessed=flops // 16, transcendentals=0),
    )(*[a for a, _ in ins])


def vmem(*arrays):
    return [(a, VMEM) for a in arrays]


def load(design):
    rows, width = design.shape
    half = width // 2

    def body(design_ref, own_ref, away_ref, sems):
        core = lax.rem(lax.axis_index("rows"), 2)
        copies = []
        for n, (side, target) in enumerate(((1 - core, away_ref), (core, own_ref))):
            source = design_ref.at[:, pl.ds(pl.multiple_of(side * half, half), half)]
            copies.append(pltpu.make_async_copy(source, target, sems.at[n]))
            copies[n].start()
        for copy in copies:
            copy.wait()

    piece = ((rows, half), design.dtype)
    ins = [(design, HBM)]
    return call(body, ins, [piece, piece], [pltpu.SemaphoreType.DMA((2,))], 0, LOAD)


def start_margins(own, away, start):
    rows, half = own.shape
    step = half // CHUNKS

    def body(own_ref, away_ref, start_ref, margins_ref, q_ref):
        core = lax.rem(lax.axis_index("rows"), 2)

        def one(i, total):
            here = pl.ds(pl.multiple_of(i * step, step), step)
            near = start_ref[:, pl.ds(pl.multiple_of(core * half + i * step, step), step)]
            far = start_ref[:, pl.ds(pl.multiple_of((1 - core) * half + i * step, step), step)]
            q_ref[:, here] = near
            for value, ref in ((near, own_ref), (far, away_ref)):
                total = total + lax.dot_general(
                    value.astype(BF16), ref[:, here], CROSS, preferred_element_type=F32
                )
            return total

        margins_ref[...] = lax.fori_loop(0, CHUNKS, one, jnp.zeros((CHAINS, rows), F32))

    outs = [((CHAINS, rows), F32), ((CHAINS, half), F32)]
    flops = 4 * CHAINS * rows * half
    return call(body, vmem(own, away, start), outs, flops=flops)


def total_of(own, one, two, three):
    return (own + two) + (one + three)


def ring_sum(partials):
    def body(own, one, two, three, out_ref):
        out_ref[...] = total_of(own[...], one[...], two[...], three[...])

    return call(body, vmem(*partials), [(partials[0].shape, F32)])[0]


def draw(labels, momenta, lag_offsets, accept_bits, step_sizes):
    rows = labels.shape[0]
    slots, width = momenta.shape[1:]
    half = width // 2

    def body(lag_ref, accept_ref, steps_ref, label_ref, bank_ref, *refs):
        mom0_ref, mom1_ref, h_ref, keep0_ref, keep1_ref, sign_ref, draws_ref, sem = refs
        core = lax.rem(lax.axis_index("rows"), 2)
        cols = pl.ds(pl.multiple_of(core * half, half), half)
        copy = pltpu.make_async_copy(bank_ref.at[:, :, cols], draws_ref, sem)
        copy.start()
        row = lax.broadcasted_iota(jnp.int32, (CHAINS, EXTRA), 0)
        h = jnp.zeros((CHAINS, EXTRA), F32)
        for k in range(PAIRS):
            h = jnp.where(row // 2 == k, steps_ref[k], h)
        h_ref[...] = h
        for s, keep_ref in enumerate((keep0_ref, keep1_ref)):
            keep = jnp.zeros((CHAINS, EXTRA), F32)
            for k in range(CHAINS):
                keep = jnp.where(row == k, accept_ref[s, k].astype(F32), keep)
            keep_ref[...] = keep
        sign_ref[...] = jnp.broadcast_to(label_ref[...].astype(F32), (8, rows))
        copy.wait()

        def pick(i, carry):
            here = pl.ds(pl.multiple_of(i * (half // 8), half // 8), half // 8)
            for s, out_ref in enumerate((mom0_ref, mom1_ref)):
                for k in range(PAIRS):
                    out_ref[2 * k : 2 * k + 1, here] = draws_ref[k, pl.ds(s + lag_ref[k], 1), here]
                    out_ref[2 * k + 1 : 2 * k + 2, here] = draws_ref[k, s : s + 1, here]
            return carry

        lax.fori_loop(0, 8, pick, 0)

    small = ((CHAINS, EXTRA), F32)
    state = ((CHAINS, half), F32)
    return call(
        body,
        [
            (lag_offsets, SMEM),
            (accept_bits, SMEM),
            (step_sizes, SMEM),
            (labels[None, :], VMEM),
            (momenta, HBM),
        ],
        [state, state, small, small, small, ((8, rows), F32)],
        [pltpu.VMEM((PAIRS, slots, half), F32), pltpu.SemaphoreType.DMA],
        0,
        8,
    )


def flip(piece):
    rows, width = piece.shape
    step = 512

    def body(piece_ref, out_ref):
        def one(i, carry):
            cols = pl.ds(pl.multiple_of(i * step, step), step)
            out_ref[cols] = piece_ref[:, cols].T
            return carry

        lax.fori_loop(0, width // step, one, 0)

    return call(body, vmem(piece), [((width, rows), piece.dtype)])[0]


def pair_start(mine, other):
    rows = mine.shape[1]

    def body(mine_ref, other_ref, margins_ref):
        margins_ref[:, :rows] = mine_ref[...]
        margins_ref[:, rows:] = other_ref[...]

    return call(body, vmem(mine, other), [((CHAINS, 2 * rows), F32)])[0]


def pair_sum(mine, other, rows):
    def body(mine_ref, other_ref, out_ref):
        out_ref[:, :rows] = mine_ref[:, :rows] + other_ref[:, rows : 2 * rows]
        out_ref[:, rows : 2 * rows] = mine_ref[:, rows : 2 * rows] + other_ref[:, :rows]
        if mine.shape[1] > 2 * rows:
            out_ref[:, 2 * rows :] = mine_ref[:, 2 * rows :] + other_ref[:, 2 * rows :]

    return call(body, vmem(mine, other), [(mine.shape, F32)])[0]


def assemble(mine, other):
    half = mine.shape[1]

    def body(mine_ref, other_ref, out_ref, sems):
        core = lax.rem(lax.axis_index("rows"), 2)
        copies = []
        for i, (ref, at) in enumerate(((mine_ref, core), (other_ref, 1 - core))):
            cols = pl.ds(pl.multiple_of(at * half, half), half)
            copies.append(pltpu.make_async_copy(ref, out_ref.at[:, cols], sems.at[i]))
            copies[-1].start()
        for copy in copies:
            copy.wait()

    return pl.pallas_call(
        body,
        in_specs=[VMEM, VMEM],
        out_specs=HBM,
        out_shape=jax.ShapeDtypeStruct((CHAINS, 2 * half), F32),
        scratch_shapes=[pltpu.SemaphoreType.DMA((2,))],
        compiler_params=limit(6),
        name="assemble",
    )(mine, other)


def square_gap(position):
    gap = position - pltpu.roll(position, CHAINS - 1, 0)
    return jnp.sum(gap * gap, axis=1, keepdims=True)


def margins_kernel(mode, pieces, arrived, h, state):
    flipped = pieces[0].shape[0] > pieces[0].shape[1]
    rows = min(pieces[0].shape)
    width = max(pieces[0].shape)
    blocks, _, block = arrived.shape
    names = list(state)
    wide = ((CHAINS, width), F32)
    outs = {"margins": ((CHAINS, 2 * rows + (EXTRA if mode == "last" else 0)), F32), "q": wide, "p": wide}
    if mode == "turn":
        outs["pos"] = wide
        outs["gap"] = ((CHAINS, EXTRA), F32)
    if mode == "last":
        outs = {"margins": outs["margins"], "base": wide, "pos": wide}

    def body(own_ref, other_ref, arrived_ref, h_ref, *refs):
        ins = dict(zip(names, refs))
        out = dict(zip(outs, refs[len(names) :]))
        h_col = h_ref[...]
        h_wide = jnp.broadcast_to(h_col[:, :1], (CHAINS, block))
        if mode in ("turn", "last"):
            keep = jnp.broadcast_to(ins["keep"][:, :1], (CHAINS, block)) != 0.0

        def one(b, cols, gap):
            g = arrived_ref[b].astype(F32)
            q = ins["q"][:, cols]
            if mode == "first":
                p = ins["mom"][:, cols] + 0.5 * h_wide * (g - q)
            elif mode == "turn":
                q0 = ins["q0"][:, cols]
                pos = jnp.where(keep, q, q0)
                gradient = jnp.where(keep, g - q, ins["g0"][b].astype(F32) - q0)
                p = ins["mom"][:, cols] + 0.5 * h_wide * gradient
                q = pos
                out["pos"][:, cols] = pos
                gap = gap + square_gap(pos)
            else:
                p = ins["p"][:, cols] + h_wide * (g - q)
            q = q + h_wide * p
            if mode == "last":
                out["base"][:, cols] = p - 0.5 * h_wide * q
            else:
                out["p"][:, cols] = p
                out["q"][:, cols] = q
            if mode == "last":
                pos = jnp.where(keep, q, ins["pos"][:, cols])
                out["pos"][:, cols] = pos
                gap = gap + square_gap(pos)
            return q.astype(BF16), gap

        def group(i, carry):
            own, other, gap = carry
            rounded = []
            for j in range(DEEP):
                b = i * DEEP + j
                part, gap = one(b, pl.ds(pl.multiple_of(b * block, block), block), gap)
                rounded.append(part)
            rounded = jnp.concatenate(rounded, axis=1)
            cols = pl.ds(pl.multiple_of(i * (DEEP * block), DEEP * block), DEEP * block)
            if flipped:
                own = own + jnp.dot(rounded, own_ref[cols], preferred_element_type=F32)
                other = other + jnp.dot(rounded, other_ref[cols], preferred_element_type=F32)
            else:
                own = own + lax.dot_general(
                    rounded, own_ref[:, cols], CROSS, preferred_element_type=F32
                )
                other = other + lax.dot_general(
                    rounded, other_ref[:, cols], CROSS, preferred_element_type=F32
                )
            return own, other, gap

        zero = jnp.zeros((CHAINS, rows), F32)
        *total, gap = lax.fori_loop(
            0, blocks // DEEP, group, (zero, zero, jnp.zeros((CHAINS, 1), F32))
        )
        if mode == "turn":
            out["gap"][...] = jnp.broadcast_to(gap, (CHAINS, EXTRA))
        if mode == "last":
            lanes = lax.broadcasted_iota(jnp.int32, (CHAINS, EXTRA), 1)
            out["margins"][:, 2 * rows :] = jnp.where(lanes == 0, ins["gap"][...], gap)
        out["margins"][:, :rows] = total[0]
        out["margins"][:, rows : 2 * rows] = total[1]

    result = call(
        body,
        vmem(*pieces, arrived, h, *state.values()),
        list(outs.values()),
        flops=4 * CHAINS * rows * width,
    )
    return dict(zip(outs, result))


def split3(column, first_lane):
    lanes = lax.broadcasted_iota(jnp.int32, (CHAINS, EXTRA), 1) - first_lane
    high = column.astype(BF16).astype(F32)
    middle = (column - high).astype(BF16).astype(F32)
    low = column - high - middle
    out = jnp.where(lanes == 0, high, jnp.zeros((CHAINS, EXTRA), F32))
    out = jnp.where(lanes == 1, middle, out)
    return jnp.where(lanes == 2, low, out)


def terms_kernel(partials, signs, held, blocks, likes, earlier):
    rows, width = held[0].shape
    block = width // blocks
    extended = earlier is not None

    def body(*refs):
        sums = [ref[...] for ref in refs[: len(partials)]]
        mine_ref, theirs_ref, near_ref, far_ref = refs[len(partials) : len(partials) + 4]
        rest = list(refs[len(partials) + 4 :])
        earlier_ref = rest.pop(0) if extended else None
        out_ref = rest.pop(0)
        total = total_of(*sums) if len(sums) > 1 else sums[0]
        sign = jnp.concatenate([mine_ref[:1], theirs_ref[:1]], axis=1)
        signed = sign * total[:, : 2 * rows]
        weights = (sign * jax.nn.sigmoid(-signed)).astype(BF16)
        if likes:
            terms = jnp.minimum(signed, 0.0) - jnp.log1p(jnp.exp(-jnp.abs(signed)))
            like = jnp.sum(terms, axis=1, keepdims=True)
            if extended:
                side = split3(earlier_ref[...][:, :1], 0) + split3(like, 3)
                side = side.astype(BF16)
                for b in range(blocks):
                    out_ref[b, :, block:] = side
                rest[0][...] = total[:, 2 * rows :]
            else:
                rest[0][...] = jnp.broadcast_to(like, (CHAINS, EXTRA))

        def group(i, carry):
            for j in range(0, WIDE, GROUP):
                at = i * WIDE + j
                cols = pl.ds(pl.multiple_of(at * block, GROUP * block), GROUP * block)
                terms = jnp.dot(weights[:, :rows], near_ref[:, cols], preferred_element_type=F32)
                far = jnp.dot(weights[:, rows:], far_ref[:, cols], preferred_element_type=F32)
                terms = (terms + far).astype(BF16)
                for b in range(GROUP):
                    out_ref[at + b, :, :block] = terms[:, b * block : (b + 1) * block]
            return carry

        lax.fori_loop(0, blocks // WIDE, group, 0)

    outs = [((blocks, CHAINS, block + (EXTRA if extended else 0)), BF16)]
    if likes:
        outs.append(((CHAINS, EXTRA), F32))
    return call(
        body,
        vmem(*partials, *signs, *held, *([earlier] if extended else [])),
        outs,
        flops=4 * CHAINS * rows * width,
    )


def sum_kernel(arrived, residual, block, likes):
    blocks = arrived.shape[0]
    carried = residual is not None

    def body(*refs):
        arrived_ref = refs[0]
        send_ref, second_ref = refs[2 if carried else 1 :]
        parts = [arrived_ref[b, :, :block].astype(F32) for b in range(blocks)]
        while len(parts) > 1:
            parts = [parts[i] + parts[i + 1] for i in range(0, len(parts), 2)]
        exact = parts[0] + refs[1][...] if carried else parts[0]
        send = exact.astype(BF16)
        if not likes:
            second_ref[...] = exact - send.astype(F32)
        for b in range(blocks):
            send_ref[b] = send
        if likes:
            side = jnp.zeros((CHAINS, EXTRA), F32)
            for b in range(blocks):
                side = side + arrived_ref[b, :, block:].astype(F32)
            second_ref[...] = side

    outs = [((blocks, CHAINS, block), BF16), ((CHAINS, EXTRA if likes else block), F32)]
    return call(body, vmem(arrived, *([residual] if carried else [])), outs)


def scores(squares, sides, observations):
    def body(square_ref, side_ref, distance_ref, like_ref):
        chain = lax.broadcasted_iota(jnp.int32, (CHAINS, PAIRS), 0)
        pair = lax.broadcasted_iota(jnp.int32, (CHAINS, PAIRS), 1)
        picked = jnp.dot(
            square_ref[...].T[:TRANS],
            (chain == 2 * pair).astype(F32),
            precision=lax.Precision.HIGHEST,
            preferred_element_type=F32,
        )
        distance_ref[...] = jnp.sqrt(picked / FEATURES + 1e-06)
        side = side_ref[...].T
        for s in range(TRANS):
            high, middle, low = (side[3 * s + i : 3 * s + i + 1] for i in range(3))
            like_ref[s : s + 1] = ((high + middle) + low) / observations

    return call(body, vmem(squares, sides), [((TRANS, PAIRS), F32), ((TRANS, CHAINS), F32)])


def finish_kernel(mine, other, half_step, base):
    blocks, _, block = mine.shape
    half = blocks * block

    def body(mine_ref, other_ref, h_ref, mine_base, other_base, out_ref, held_ref, sems):
        core = lax.rem(lax.axis_index("rows"), 2)
        step = 0.5 * jnp.broadcast_to(h_ref[...][:, :1], (CHAINS, block))
        copies = []
        for n, (side, ref, base_ref) in enumerate(
            ((core, mine_ref, mine_base), (1 - core, other_ref, other_base))
        ):

            def one(i, carry):
                for j in range(GROUP):
                    b = i * GROUP + j
                    cols = pl.ds(pl.multiple_of(b * block, block), block)
                    held_ref[n, :, cols] = base_ref[:, cols] + step * ref[b].astype(F32)
                return carry

            lax.fori_loop(0, blocks // GROUP, one, 0)
            target = out_ref.at[:, pl.ds(pl.multiple_of(side * half, half), half)]
            copies.append(pltpu.make_async_copy(held_ref.at[n], target, sems.at[n]))
            copies[n].start()
        for copy in copies:
            copy.wait()

    return pl.pallas_call(
        body,
        in_specs=[VMEM] * 5,
        out_specs=HBM,
        out_shape=jax.ShapeDtypeStruct((CHAINS, 2 * half), F32),
        scratch_shapes=[pltpu.VMEM((2, CHAINS, half), F32), pltpu.SemaphoreType.DMA((2,))],
        compiler_params=limit(6),
        name="finish",
    )(mine, other, half_step, *base)


def on_device(design, labels, start_position, momenta, lag_offsets, accept_bits, step_sizes):
    rows, _ = design.shape
    devices = lax.axis_size("rows")
    ring = lax.axis_size("feat")
    blocks = devices // 2
    chips = [[2 * k + core for k in range(blocks)] for core in range(2)]
    swap = [(i, i ^ 1) for i in range(devices)]

    def exchange(blocked):
        return lax.all_to_all(blocked, "rows", 0, 0, axis_index_groups=chips)

    def across(value):
        return lax.ppermute(value, "rows", swap)

    def around(margins):
        moved = {}
        for k in (2, 1, 3):
            pairs = [(i, (i + k) % ring) for i in range(ring)]
            moved[k] = lax.ppermute(margins, "feat", pairs)
        return [margins, moved[1], moved[2], moved[3]]

    def gradient(partials, residual, likes=False, earlier=None, beside=()):
        last = earlier is not None
        out, *side = terms_kernel(partials, signs, held, blocks, likes, earlier)
        out, *beside = lax.optimization_barrier((out, *beside))
        block = out.shape[2] - (EXTRA if last else 0)
        send, second = sum_kernel(exchange(out), residual, block, last)
        residual, totals = (None, [second]) if last else (second, [])
        return exchange(send), residual, side + totals + beside

    def paired(margins):
        return around(pair_sum(margins, across(margins), rows))

    own, away = load(design)
    held = (own, across(away))
    margins, start = start_margins(own, away, start_position)
    mom0, mom1, h, keep0, keep1, sign = draw(labels, momenta, lag_offsets, accept_bits, step_sizes)
    partials, signs = lax.optimization_barrier((around(margins), (sign, across(sign))))
    sign = signs[0]
    margins = ring_sum(partials)
    margins = pair_start(margins, across(margins))
    g0, residual, (mom0, mom1) = gradient([margins], None, beside=(mom0, mom1))
    g = g0
    pieces = held
    flips = []
    now = {"q": start}
    for leap in range(LEAP):
        if leap == 0:
            now = margins_kernel("first", pieces, g, h, {"q": start, "mom": mom0})
        else:
            now = margins_kernel("mid", pieces, g, h, {"q": now["q"], "p": now["p"]})
        partials = paired(now["margins"])
        beside = (flip(held[leap]),) if leap < len(held) else ()
        g, residual, side = gradient(partials, residual, leap + 1 == LEAP, beside=beside)
        if beside:
            flips += side
        if len(flips) == len(held):
            pieces = tuple(flips)
    (like,) = side
    for leap in range(LEAP):
        last = leap + 1 == LEAP
        if leap == 0:
            state = {"q": now["q"], "q0": start, "g0": g0, "mom": mom1, "keep": keep0}
            now = margins_kernel("turn", pieces, g, h, state)
            position, gap = now["pos"], now["gap"]
        elif not last:
            now = margins_kernel("mid", pieces, g, h, {"q": now["q"], "p": now["p"]})
        else:
            state = {"q": now["q"], "p": now["p"], "pos": position, "gap": gap, "keep": keep1}
            now = margins_kernel("last", pieces, g, h, state)
            swapped, position, base = lax.optimization_barrier(
                (across(now["margins"]), now["pos"], now["base"])
            )
            partials = around(pair_sum(now["margins"], swapped, rows))
            final_position = assemble(position, across(position))
            base = (base, across(base))
            sign, final_position, base = lax.optimization_barrier((sign, final_position, base))
            signs = (sign, signs[1])
        if not last:
            partials = paired(now["margins"])
        g, residual, side = gradient(partials, residual, last, like if last else None)
    squares, sides = side
    g, squares, sides = lax.optimization_barrier((g, squares, sides))
    distances, likes = scores(squares, sides, rows * devices)
    momentum = finish_kernel(g, across(g), h, base)
    return (final_position, momentum, likes, distances)


def solution(mesh):
    return jax.shard_map(
        on_device,
        mesh=mesh,
        in_specs=(
            P("rows", "feat"),
            P("rows"),
            P(None, "feat"),
            P(None, None, "feat"),
            P(),
            P(),
            P(),
        ),
        out_specs=(P(None, "feat"), P(None, "feat"), P(), P()),
        check_vma=False,
    )
```
